128 devices in a mesh: ctx: 128 (over x, y, z, core).
Axes of the slice: x: 4, y: 4, z: 4, core: 2. Of those that a mesh axis runs over, the one named last changes fastest.
Arguments:
- queries: bfloat16 [32768, 2048], P('ctx')
- keys: bfloat16 [32768, 512], P('ctx')
- values: bfloat16 [32768, 512], P('ctx'), may hold values from -6 to 6
- cotangent: bfloat16 [32768, 2048], P('ctx'), may hold values from -180 to 180
- summary_positions: int32 [256], replicated, may hold values from 0 to 32767, as said below
Outputs:
- query_grad: bfloat16 [32768, 2048], P('ctx')
- key_grad: bfloat16 [32768, 512], P('ctx')
- value_gradient: bfloat16 [32768, 512], P('ctx')
The draws below stay inside these ranges and needn't reach their ends.
Inputs may be any that keep to these rules, and one draw needn't show every extreme that they name: `summary_positions`: entry m lies in [m * 128, (m + 1) * 128); the first entry is 0 and the last is 32767.
All inputs are finite; a program needn't handle non-finite values.
Results may differ from the reference program's by a relative error of at most 0.012.
The reference program's roundings to bfloat16 on the way count: a program that leaves them out, or rounds other values in their place, can miss the bound.
Values may be sent and summed in bfloat16 or wider, within the bound.
No kernel may reach another device: no remote copies, remote signals or barrier semaphores. Data moves between devices by JAX's collectives and lax.ppermute only.
A program may use at most 128 MiB of HBM per device.

```python
import jax
import jax.numpy as jnp
from jax import lax

HQ = 16
HK = 4
HEAD = 128
STRIDE = 128
BAND_LENGTH = 1024
TOK_DEV = 256
TOKENS = 32768
NSUM = 256


def draw_queries(key, part):
    noise_key = jax.random.fold_in(key, 21)
    noise = jax.random.normal(noise_key, (TOKENS, HQ * HEAD), jnp.float32)
    return noise.astype(jnp.bfloat16)


def draw_keys(key, part):
    noise_key = jax.random.fold_in(key, 31)
    noise = jax.random.normal(noise_key, (TOKENS, HK * HEAD), jnp.float32)
    return noise.astype(jnp.bfloat16)


def draw_summary_positions(key, part):
    inside = jax.random.randint(jax.random.fold_in(key, 41), (NSUM,), 0, STRIDE, dtype=jnp.int32)
    entries = jnp.arange(NSUM, dtype=jnp.int32)
    inside = jnp.where(entries == 0, 0, inside)
    inside = jnp.where(entries == NSUM - 1, STRIDE - 1, inside)
    return entries * STRIDE + inside


def shard_levels(stream_key, extent, pieces, least, largest):
    def one(position, shards_of):
        heights = jax.random.uniform(jax.random.fold_in(jax.random.fold_in(stream_key, 6), position), (shards_of,), jnp.float32, least / len(pieces), largest / len(pieces))
        return jnp.repeat(jnp.exp(heights), extent[position] // shards_of).reshape((-1,) + (1,) * (len(extent) - position - 1))

    factor_of = one(*pieces[0])
    for cut in pieces[1:]:
        factor_of = factor_of * one(*cut)
    return factor_of


def scatter_about(own_key, extent, deviation, most, split=(), held_as=jnp.bfloat16):
    values = deviation * jax.random.normal(own_key, extent, jnp.float32)
    if split:
        values = values * shard_levels(own_key, extent, split, -0.22, 0.18)
    return jnp.clip(values, -most, most).astype(held_as)


def setup_inputs(seed: int = 0) -> dict:
    splits = jax.random.split(jax.random.key(seed), 6)
    queries = draw_queries(jax.random.fold_in(splits[5], 71), 0)
    keys = draw_keys(jax.random.fold_in(splits[5], 71), 0)
    values = scatter_about(splits[2], (TOKENS, HK * HEAD), 1.0, 6.0, ((0, 128),))
    cotangent = scatter_about(splits[3], (TOKENS, HQ * HEAD), 30.0, 180.0, ((0, 128),))
    summary_positions = draw_summary_positions(jax.random.fold_in(splits[5], 71), 0)
    return dict(queries=queries, keys=keys, values=values, cotangent=cotangent, summary_positions=summary_positions)


NEGATIVE = -1e30


def reference(queries, keys, values, cotangent, summary_positions):
    tokens, qcols = queries.shape
    kcols = keys.shape[1]
    kv_heads = kcols // HEAD
    group = qcols // kcols
    scale = HEAD ** -0.5
    window = BAND_LENGTH + TOK_DEV
    summ_count = summary_positions.shape[0]
    summ_keys = jnp.take(keys, summary_positions, axis=0).astype(jnp.float32).reshape(summ_count, kv_heads, HEAD)
    summ_vals = jnp.take(values, summary_positions, axis=0).astype(jnp.float32).reshape(summ_count, kv_heads, HEAD)
    zero_rows = jnp.zeros((BAND_LENGTH, kcols), keys.dtype)
    padded_k = jnp.concatenate([zero_rows, keys], 0)
    padded_v = jnp.concatenate([zero_rows, values], 0)

    def block_step(loop_state, block):
        key_gradient_total, value_gradient_total, summary_key_gradient, summary_value_gradient = loop_state
        start = (block * TOK_DEV).astype(jnp.int32)
        query_blk = lax.dynamic_slice_in_dim(queries, start, TOK_DEV, 0).astype(jnp.float32).reshape(TOK_DEV, kv_heads, group, HEAD)
        cot_blk = lax.dynamic_slice_in_dim(cotangent, start, TOK_DEV, 0).astype(jnp.float32).reshape(TOK_DEV, kv_heads, group, HEAD)
        band_keys = lax.dynamic_slice_in_dim(padded_k, start, window, 0).astype(jnp.float32).reshape(window, kv_heads, HEAD)
        band_vals = lax.dynamic_slice_in_dim(padded_v, start, window, 0).astype(jnp.float32).reshape(window, kv_heads, HEAD)
        query_pos = start + jnp.arange(TOK_DEV, dtype=jnp.int32)
        band_pos = start - BAND_LENGTH + jnp.arange(window, dtype=jnp.int32)
        distance = query_pos[:, None] - band_pos[None, :]
        band_mask = (distance >= 0) & (distance < BAND_LENGTH) & (band_pos[None, :] >= 0)
        summ_mask = summary_positions[None, :] <= query_pos[:, None]
        band_score = jnp.einsum('thgd,khd->hgtk', query_blk, band_keys) * scale
        band_score = jnp.where(band_mask, band_score, NEGATIVE)
        summ_score = jnp.einsum('thgd,khd->hgtk', query_blk, summ_keys) * scale
        summ_score = jnp.where(summ_mask, summ_score, NEGATIVE)
        highest = jnp.maximum(jnp.max(band_score, -1), jnp.max(summ_score, -1))
        total = jnp.sum(jnp.exp(band_score - highest[..., None]), -1) + jnp.sum(jnp.exp(summ_score - highest[..., None]), -1)
        log_total = highest + jnp.log(total)
        band_prob = jnp.exp(band_score - log_total[..., None])
        summ_prob = jnp.exp(summ_score - log_total[..., None])
        band_half = lax.optimization_barrier(band_prob.astype(jnp.bfloat16)).astype(jnp.float32)
        summ_half = lax.optimization_barrier(summ_prob.astype(jnp.bfloat16)).astype(jnp.float32)
        attended = jnp.einsum('hgtk,khd->thgd', band_half, band_vals) + jnp.einsum('hgtk,khd->thgd', summ_half, summ_vals)
        attended = lax.optimization_barrier(attended.astype(jnp.bfloat16)).astype(jnp.float32)
        delta = jnp.einsum('thgd,thgd->hgt', cot_blk, attended)
        band_dprob = jnp.einsum('thgd,khd->hgtk', cot_blk, band_vals)
        summ_dprob = jnp.einsum('thgd,khd->hgtk', cot_blk, summ_vals)
        band_dscore = lax.optimization_barrier((band_prob * (band_dprob - delta[..., None])).astype(jnp.bfloat16)).astype(jnp.float32)
        summ_dscore = lax.optimization_barrier((summ_prob * (summ_dprob - delta[..., None])).astype(jnp.bfloat16)).astype(jnp.float32)
        query_grad = (jnp.einsum('hgtk,khd->thgd', band_dscore, band_keys) + jnp.einsum('hgtk,khd->thgd', summ_dscore, summ_keys)) * scale
        key_band = (jnp.einsum('hgtk,thgd->khd', band_dscore, query_blk) * scale).reshape(window, kcols)
        val_band = jnp.einsum('hgtk,thgd->khd', band_half, cot_blk).reshape(window, kcols)
        summary_key_rows = (jnp.einsum('hgtk,thgd->khd', summ_dscore, query_blk) * scale).reshape(summ_count, kcols)
        summary_value_rows = jnp.einsum('hgtk,thgd->khd', summ_half, cot_blk).reshape(summ_count, kcols)
        key_window = lax.dynamic_slice_in_dim(key_gradient_total, start, window, 0) + key_band
        val_window = lax.dynamic_slice_in_dim(value_gradient_total, start, window, 0) + val_band
        key_gradient_total = lax.dynamic_update_slice_in_dim(key_gradient_total, key_window, start, 0)
        value_gradient_total = lax.dynamic_update_slice_in_dim(value_gradient_total, val_window, start, 0)
        updated_state = (key_gradient_total, value_gradient_total, summary_key_gradient + summary_key_rows, summary_value_gradient + summary_value_rows)
        return updated_state, query_grad.reshape(TOK_DEV, qcols).astype(jnp.bfloat16)

    start_carry = (jnp.zeros((tokens + BAND_LENGTH, kcols), jnp.float32), jnp.zeros((tokens + BAND_LENGTH, kcols), jnp.float32),
                   jnp.zeros((summ_count, kcols), jnp.float32), jnp.zeros((summ_count, kcols), jnp.float32))
    final_state, query_blocks = lax.scan(block_step, start_carry, jnp.arange(tokens // TOK_DEV, dtype=jnp.int32))
    key_gradient_total, value_gradient_total, summary_key_gradient, summary_value_gradient = final_state
    query_grad = query_blocks.reshape(tokens, qcols)
    key_grad = key_gradient_total[BAND_LENGTH:].at[summary_positions].add(summary_key_gradient)
    value_gradient = value_gradient_total[BAND_LENGTH:].at[summary_positions].add(summary_value_gradient)
    return query_grad, key_grad.astype(jnp.bfloat16), value_gradient.astype(jnp.bfloat16)
```

```python
import jax, jax.numpy as jnp
from jax import lax
from jax.experimental import pallas as pl
from jax.experimental.pallas import tpu as pltpu
from jax.sharding import PartitionSpec as P
HEAD=128; BAND=1024; R=256; NS=256
BIG = 3e38
NEG = -1e30
SCALE=HEAD**-0.5
LOG2E=1.4426950408889634
F32=jnp.float32; BF=jnp.bfloat16
def dot(a,b): return jnp.dot(a,b,preferred_element_type=F32)

def kernel(where_ref, pos_ref, qo_ref, qs_ref, do_ref, ds_ref, kv2_ref, kv1_ref, kv0_ref, sm_ref,
           dqo_ref, dqs_ref, g2_ref, g1_ref, g0_ref, gs_ref,
           k_sc, v_sc, kt_sc, vt_sc, s_sc, p16_sc, dk_sc, dv_sc, lima_sc, limb_sc):
    chip=where_ref[0]; core=where_ref[1]
    for i,r in enumerate((kv2_ref,kv1_ref,kv0_ref,sm_ref)):
        n=r.shape[0]
        k=r[:, :HEAD]; v=r[:, HEAD:]
        k_sc[pl.ds(i*512,n),:]=k; v_sc[pl.ds(i*512,n),:]=v
        kt_sc[:, pl.ds(i*512,n)]=k.T; vt_sc[:, pl.ds(i*512,n)]=v.T
    ki=lax.broadcasted_iota(jnp.int32,(R,R),0); qi=lax.broadcasted_iota(jnp.int32,(R,R),1)
    lima_sc[...]=jnp.where(ki>qi,BIG,NEG); limb_sc[...]=jnp.where(ki<=qi,BIG,NEG)
    dk_sc[...]=jnp.zeros_like(dk_sc); dv_sc[...]=jnp.zeros_like(dv_sc)
    c=SCALE*LOG2E
    for side,(q_ref,d_ref,dq_ref) in enumerate(((qo_ref,do_ref,dqo_ref),(qs_ref,ds_ref,dqs_ref))):
        b = core if side==0 else 1-core
        off=[pl.multiple_of(b*R+t*R,R) for t in range(5)]+[1536]
        qpos=(chip*2+b)*R+qi
        lims=jnp.where(pos_ref[...]<=qpos,BIG,NEG)
        qt=[q_ref[:,h*HEAD:(h+1)*HEAD].T for h in range(4)]
        dt=[d_ref[:,h*HEAD:(h+1)*HEAD].T for h in range(4)]
        for t in range(6):
            kk=k_sc[pl.ds(off[t],R),:]
            for h in range(4):
                s=dot(kk,qt[h])
                if t==0: s=jnp.minimum(s,lima_sc[...])
                if t==4: s=jnp.minimum(s,limb_sc[...])
                if t==5: s=jnp.minimum(s,lims)
                s_sc[t*R:(t+1)*R,h*R:(h+1)*R]=s
        @pl.when(chip<2)
        def _():
            for t in range(4):
                @pl.when(chip*2+b+t<4)
                def _():
                    s_sc[t*R:(t+1)*R,:]=jnp.full((R,1024),NEG,F32)
        for h in range(4):
            hs=slice(h*R,(h+1)*R)
            m=jnp.max(s_sc[:,hs],axis=0,keepdims=True)
            m2=m*c
            l=jnp.zeros((1,R),F32)
            for t in range(6):
                p=jnp.exp2(s_sc[t*R:(t+1)*R,hs]*c-m2)
                s_sc[t*R:(t+1)*R,hs]=p
                l=l+jnp.sum(p,axis=0,keepdims=True)
            inv=1.0/l
            o=jnp.zeros((HEAD,R),F32)
            for t in range(6):
                p=s_sc[t*R:(t+1)*R,hs]*inv
                p16=p.astype(BF)
                p16_sc[t*R:(t+1)*R,hs]=p16
                o=o+dot(vt_sc[:,pl.ds(off[t],R)],p16)
            att=o.astype(BF).astype(F32)
            delta=jnp.sum(dt[h].astype(F32)*att,axis=0,keepdims=True)
            dq=jnp.zeros((HEAD,R),F32)
            for t in range(6):
                dp=dot(v_sc[pl.ds(off[t],R),:],dt[h])
                p=s_sc[t*R:(t+1)*R,hs]*inv
                d=(p*(dp-delta)).astype(BF)
                dk_sc[pl.ds(off[t],R),:]+=dot(d,q_ref[:,h*HEAD:(h+1)*HEAD])
                dv_sc[pl.ds(off[t],R),:]+=dot(p16_sc[t*R:(t+1)*R,hs],d_ref[:,h*HEAD:(h+1)*HEAD])
                dq=dq+dot(kt_sc[:,pl.ds(off[t],R)],d)
            dq_ref[:,h*HEAD:(h+1)*HEAD]=(dq*SCALE).T.astype(BF)
    for i,r in enumerate((g2_ref,g1_ref,g0_ref,gs_ref)):
        n=r.shape[0]
        r[:, :HEAD]=(dk_sc[pl.ds(i*512,n),:]*SCALE).astype(r.dtype)
        r[:, HEAD:]=dv_sc[pl.ds(i*512,n),:].astype(r.dtype)

def attend(where,pos,qo,qs,do,ds,kv2,kv1,kv0,sm):
    vm=pl.BlockSpec(memory_space=pltpu.VMEM)
    sds=jax.ShapeDtypeStruct
    return pl.pallas_call(kernel,
        in_specs=[pl.BlockSpec(memory_space=pltpu.SMEM)]+[vm]*9,
        out_specs=[vm]*6,
        out_shape=[sds((R,512),BF),sds((R,512),BF),sds((512,256),BF),sds((512,256),BF),sds((512,256),F32),sds((NS,256),F32)],
        scratch_shapes=[pltpu.VMEM((1792,HEAD),BF),pltpu.VMEM((1792,HEAD),BF),pltpu.VMEM((HEAD,1792),BF),pltpu.VMEM((HEAD,1792),BF),
            pltpu.VMEM((1536,1024),F32),pltpu.VMEM((1536,1024),BF),pltpu.VMEM((1792,HEAD),F32),pltpu.VMEM((1792,HEAD),F32),
            pltpu.VMEM((R,R),F32),pltpu.VMEM((R,R),F32)],
        compiler_params=pltpu.CompilerParams(vmem_limit_bytes=48<<20),
        cost_estimate=pl.CostEstimate(flops=5_000_000_000,bytes_accessed=4_000_000,transcendentals=3_000_000),
        name="attend")(where,pos,qo,qs,do,ds,kv2,kv1,kv0,sm)


def to_sibling(block):
    return lax.ppermute(block, "ctx", [(i, i ^ 1) for i in range(lax.axis_size("ctx"))])


def to_chip(block, hops):
    size = lax.axis_size("ctx")
    route = [(i, i + 2 * hops) for i in range(size) if 0 <= i + 2 * hops < size]
    return lax.ppermute(block, "ctx", route)


def exchange(block):
    chips = lax.axis_size("ctx") // 2
    groups = [[2 * i + k for i in range(chips)] for k in range(2)]
    return lax.all_to_all(block, "ctx", 0, 0, axis_index_groups=groups, tiled=True)


def in_order(core, own, sibling, axis):
    return jnp.where(
        core == 0,
        jnp.concatenate([own, sibling], axis),
        jnp.concatenate([sibling, own], axis),
    )


def columns(block, start, size):
    return lax.dynamic_slice_in_dim(block, start, size, 1)


def body(queries, keys, values, cotangent, summary_positions):
    rows = queries.shape[0]
    index = lax.axis_index("ctx")
    chips = lax.axis_size("ctx") // 2
    chip, core = index // 2, index % 2
    half = 2 * HEAD

    def halves(which):
        parts = []
        for g in range(2):
            start = (2 * which + g) * HEAD
            parts += [columns(keys, start, HEAD), columns(values, start, HEAD)]
        return jnp.concatenate(parts, 1)

    kv_own = halves(core)
    kv_sib = to_sibling(halves(1 - core))
    qd_sib = to_sibling(
        jnp.concatenate(
            [columns(queries, (1 - core) * 1024, 1024), columns(cotangent, (1 - core) * 1024, 1024)], 1
        )
    )
    q_own = columns(queries, core * 1024, 1024)
    d_own = columns(cotangent, core * 1024, 1024)
    kv0 = in_order(core, kv_own, kv_sib, 0)
    per_chip = summary_positions.shape[0] // chips
    local = lax.dynamic_slice_in_dim(summary_positions, chip * per_chip, per_chip, 0) - chip * 2 * rows
    pick = (local[:, None] == jnp.arange(2 * rows, dtype=jnp.int32)[None, :])
    picked = jnp.dot(pick.astype(BF), kv0, preferred_element_type=F32).astype(BF)
    summ = exchange(jnp.broadcast_to(picked[None], (chips, per_chip, 2 * half)))
    summ = summ.reshape(chips * per_chip, 2 * half)
    where = jnp.stack([chip, core]).astype(jnp.int32)
    pos = summary_positions[:, None]
    kv0_g = [kv0[:, g * half : (g + 1) * half] for g in range(2)]
    kv1_g, kv2_g = [], []
    for g in range(2):
        kv1_g.append(to_chip(kv0_g[g], 1))
        kv2_g.append(to_chip(kv0_g[g], 2))
    totals, dq_own, dq_sib = [], [], []
    for g in range(2):
        cols = slice(g * 512, (g + 1) * 512)
        sib_cols = slice(1024 + g * 512, 1024 + (g + 1) * 512)
        dqo, dqs, back2, back1, own, summ_grad = attend(
            where, pos, q_own[:, cols], qd_sib[:, cols], d_own[:, cols], qd_sib[:, sib_cols],
            kv2_g[g], kv1_g[g], kv0_g[g], summ[:, g * half : (g + 1) * half],
        )
        dq_own.append(dqo)
        dq_sib.append(dqs)
        shares = exchange(summ_grad.reshape(chips, per_chip, half))
        share = jnp.sum(shares, 0)
        back2 = to_chip(back2, -2)
        back1 = to_chip(back1, -1)
        placed = jnp.dot(pick.T.astype(F32), share, precision=lax.Precision.HIGHEST)
        totals.append(own + back1.astype(F32) + back2.astype(F32) + placed)
    dq_recv = to_sibling(jnp.concatenate(dq_sib, 1))
    query_grad = in_order(core, jnp.concatenate(dq_own, 1), dq_recv, 1)
    total = jnp.concatenate([totals[0][:, :HEAD], totals[1][:, :HEAD], totals[0][:, HEAD:], totals[1][:, HEAD:]], 1).astype(BF)
    mine = lax.dynamic_slice_in_dim(total, core * rows, rows, 0)
    recv = to_sibling(lax.dynamic_slice_in_dim(total, (1 - core) * rows, rows, 0))
    key_grad = in_order(core, mine[:, :half], recv[:, :half], 1)
    value_gradient = in_order(core, mine[:, half:], recv[:, half:], 1)
    return query_grad, key_grad, value_gradient


def solution(mesh):
    return jax.shard_map(
        body,
        mesh=mesh,
        in_specs=(P("ctx", None), P("ctx", None), P("ctx", None), P("ctx", None), P()),
        out_specs=(P("ctx", None), P("ctx", None), P("ctx", None)),
        check_vma=False,
    )
```

```python
import functools

import jax
import jax.numpy as jnp
from jax import lax
from jax.experimental import pallas as pl
from jax.experimental.pallas import tpu as pltpu
from jax.sharding import PartitionSpec as P

HEAD = 128
ROWS = 256
SPAN = 1792
GATHER_FLOPS = 6_000_000_000
UNPACK_FLOPS = 40_000_000_000
BIG = 3e38
NEG = -1e30
SCALE = HEAD**-0.5
LOG2E = 1.4426950408889634
F32 = jnp.float32
BF = jnp.bfloat16
VM = pl.BlockSpec(memory_space=pltpu.VMEM)
SM = pl.BlockSpec(memory_space=pltpu.SMEM)
ANY = pl.BlockSpec(memory_space=pltpu.HBM)


def dot(a, b):
    return jnp.dot(a, b, preferred_element_type=F32)


def place():
    index = lax.axis_index("ctx")
    return index, index // 2, index % 2


def window(start, size):
    return pl.ds(pl.multiple_of(start, size), size)


def run(copies):
    for copy in copies:
        copy.start()
    for copy in copies:
        copy.wait()


def pack_kernel(pos_ref, k_ref, v_ref, q_hbm, d_hbm, own_ref, send_ref, block_ref, qd_ref, sem):
    index, _, core = place()
    copies = []
    for i, ref in enumerate((q_hbm, d_hbm)):
        src = ref.at[:, window((1 - core) * 1024, 1024)]
        copies.append(pltpu.make_async_copy(src, qd_ref.at[:, i * 1024 : (i + 1) * 1024], sem.at[i]))
        copies[-1].start()
    for out, which in ((own_ref, core), (send_ref, 1 - core)):
        for g in range(2):
            cols = window((2 * which + g) * HEAD, HEAD)
            out[g, :, :HEAD] = k_ref[:, cols]
            out[g, :, HEAD:] = v_ref[:, cols]
    slot = lax.broadcasted_iota(jnp.int32, (8, ROWS), 0)
    row = lax.broadcasted_iota(jnp.int32, (8, ROWS), 1)
    first = pos_ref[2 * index] - index * ROWS
    second = pos_ref[2 * index + 1] - index * ROWS
    wanted = jnp.where(slot % 2 == 0, first, second)
    tiles = []
    for which in range(2):
        tile = jnp.zeros((8, HEAD), F32)
        for g in range(2):
            for i, ref in enumerate((k_ref, v_ref)):
                pick = ((row == wanted) & (slot // 2 == 2 * g + i)).astype(F32).astype(BF)
                head = 2 * which + g
                tile = tile + dot(pick, ref[:, head * HEAD : (head + 1) * HEAD])
        tiles.append(tile.astype(BF))
    for device in range(block_ref.shape[0]):
        block_ref[device] = tiles[device % 2]
    for copy in copies:
        copy.wait()


def pack(pos, keys, values, queries, cotangent):
    shape = jax.ShapeDtypeStruct
    return pl.pallas_call(
        pack_kernel,
        in_specs=[SM, VM, VM, ANY, ANY],
        out_specs=[VM] * 4,
        out_shape=[
            shape((2, ROWS, 2 * HEAD), BF),
            shape((2, ROWS, 2 * HEAD), BF),
            shape((128, 8, HEAD), BF),
            shape((ROWS, 2048), BF),
        ],
        scratch_shapes=[pltpu.SemaphoreType.DMA((2,))],
        compiler_params=pltpu.CompilerParams(vmem_limit_bytes=60 << 20),
        name="pack",
    )(pos, keys, values, queries, cotangent)


def unpack_kernel(pos_ref, summ_ref, sk0_ref, sk1_ref, posb_ref, f_sc, t_sc):
    f_sc[...] = summ_ref[...].astype(F32)
    for g, out in enumerate((sk0_ref, sk1_ref)):
        for i in range(2):
            for r in range(2):
                slots = pl.ds(4 * g + 2 * i + r, 128, stride=8)
                t_sc[pl.ds(r, 128, stride=2), :] = f_sc[slots, :]
            out[:, i * HEAD : (i + 1) * HEAD] = t_sc[...].astype(BF)
    for i in range(2):
        row = jnp.broadcast_to(pos_ref[i : i + 1, :].astype(F32), (HEAD, HEAD))
        posb_ref[i * HEAD : (i + 1) * HEAD, :] = row.T


def unpack(pos, summ):
    shape = jax.ShapeDtypeStruct
    return pl.pallas_call(
        unpack_kernel,
        in_specs=[VM, VM],
        out_specs=[VM] * 3,
        out_shape=[shape((ROWS, 256), BF), shape((ROWS, 256), BF), shape((ROWS, HEAD), F32)],
        scratch_shapes=[pltpu.VMEM((1024, HEAD), F32), pltpu.VMEM((ROWS, HEAD), F32)],
        compiler_params=pltpu.CompilerParams(vmem_limit_bytes=60 << 20),
        cost_estimate=pl.CostEstimate(flops=UNPACK_FLOPS, bytes_accessed=1_000_000, transcendentals=0),
        name="unpack",
    )(pos, summ)


def fold(x, op):
    return op(x.reshape(x.shape[0] // 8, 8, x.shape[1]), axis=0)


def attend_kernel(g, pos_ref, q_hbm, d_hbm, qd_hbm, kv2, kv1, kv0, summ, *rest):
    before, rest = (rest[0], rest[1:]) if g else (None, rest)
    dqo_hbm, dqs_hbm, gs_hbm, grad_hbm = rest[0], rest[1], rest[2], rest[3:6]
    (k_sc, v_sc, kt_sc, vt_sc, s_sc, q_sc, d_sc, dq_sc, dk_sc, dv_sc, lim_sc, lims_sc) = rest[6:18]
    own_sc, bf_sc, gs_sc, sem, out_sem = rest[18:]
    _, chip, core = place()
    mine = window(core * ROWS, ROWS)
    theirs = window((1 - core) * ROWS, ROWS)
    copies = []

    def copy(src, dst):
        copies.append(pltpu.make_async_copy(src, dst, sem.at[len(copies)]))
        copies[-1].start()

    if g:
        copy(before, gs_sc)
    copy(q_hbm.at[:, window(core * 1024 + g * 512, 512)], q_sc.at[mine])
    copy(d_hbm.at[:, window(core * 1024 + g * 512, 512)], d_sc.at[mine])
    copy(qd_hbm.at[:, g * 512 : (g + 1) * 512], q_sc.at[theirs])
    copy(qd_hbm.at[:, 1024 + g * 512 : 1536 + g * 512], d_sc.at[theirs])
    for i, kv in enumerate((kv2, kv1, kv0)):
        for part in range(2):
            at = window(i * 512 + (core if part == 0 else 1 - core) * ROWS, ROWS)
            rows = slice(part * ROWS, (part + 1) * ROWS)
            copy(kv.at[rows, :HEAD], k_sc.at[at])
            copy(kv.at[rows, HEAD:], v_sc.at[at])
    copy(summ.at[:, :HEAD], k_sc.at[1536:])
    copy(summ.at[:, HEAD:], v_sc.at[1536:])
    ki = lax.broadcasted_iota(jnp.int32, (ROWS, ROWS), 0)
    qi = lax.broadcasted_iota(jnp.int32, (ROWS, ROWS), 1)
    pos = jnp.concatenate([pos_ref[...], pos_ref[...]], 1)
    for b in range(2):
        lim_sc[b] = jnp.where((ki > qi) & (chip * 2 + b >= 4), BIG, NEG)
        lims_sc[b] = jnp.where(pos <= ((chip * 2 + b) * ROWS + qi).astype(F32), BIG, NEG)
    lim_sc[2] = jnp.where(ki <= qi, BIG, NEG)
    dk_sc[...] = jnp.zeros_like(dk_sc)
    dv_sc[...] = jnp.zeros_like(dv_sc)
    for done in copies:
        done.wait()
    for i in range(7):
        at = slice(i * ROWS, (i + 1) * ROWS)
        kt_sc[:, at] = k_sc[at, :].T
        vt_sc[:, at] = v_sc[at, :].T
    outs = []

    def send(src, dst):
        outs.append(pltpu.make_async_copy(src, dst, out_sem.at[len(outs)]))
        outs[-1].start()

    def emit():
        send(dq_sc.at[mine], dqo_hbm)
        send(dq_sc.at[theirs], dqs_hbm)
        dk_sc[1536:, :] = dk_sc[1536:, :] * SCALE
        for i, acc in enumerate((dk_sc, dv_sc)):
            for r in range(2):
                slots = pl.ds(4 * g + 2 * i + r, 128, stride=8)
                gs_sc[slots, :] = acc[pl.ds(1536 + r, 128, stride=2), :]
        send(gs_sc, gs_hbm)
        for i, hbm in enumerate(grad_hbm):
            for part in range(2):
                at = window((2 - i) * 512 + (core if part == 0 else 1 - core) * ROWS, ROWS)
                rows = slice(part * ROWS, (part + 1) * ROWS)
                stage, kind = (own_sc, F32) if i == 0 else (bf_sc.at[i - 1], BF)
                stage[rows, :HEAD] = (dk_sc[at, :] * SCALE).astype(kind)
                stage[rows, HEAD:] = dv_sc[at, :].astype(kind)
            send(stage, hbm)

    factor = SCALE * LOG2E

    def base(u, t):
        return 1536 if t == 5 else (u["b"] + t) * ROWS

    units = [dict(b=u // 4, h=u % 4, slot=u % 3) for u in range(8)]

    def open_unit(u):
        rows = slice(u["b"] * ROWS, (u["b"] + 1) * ROWS)
        cols = slice(u["h"] * HEAD, (u["h"] + 1) * HEAD)
        u["q"], u["d"] = q_sc[rows, cols], d_sc[rows, cols]
        u["qt"], u["dt"] = u["q"].T, u["d"].T
        u["m"] = u["l"] = u["o"] = u["dq"] = None

    def scores(u, t):
        b, at = u["b"], slice(t * ROWS, (t + 1) * ROWS)
        s = dot(k_sc[base(u, t) : base(u, t) + ROWS, :], u["qt"])
        if t == 0:
            limit = lim_sc[b]
        elif t == 4:
            limit = lim_sc[2]
        elif t == 5:
            limit = lims_sc[b]
        else:
            limit = jnp.where(chip * 2 + b + t >= 4, BIG, NEG)
        s = jnp.minimum(s, limit)
        s_sc[u["slot"], at, :] = s
        m = fold(s, jnp.max)
        u["m"] = m if u["m"] is None else jnp.maximum(u["m"], m)

    def close_scores(u):
        u["m2"] = jnp.max(u["m"], axis=0, keepdims=True) * factor

    def weights(u, t):
        b, at = u["b"], slice(t * ROWS, (t + 1) * ROWS)
        p = jnp.exp2(s_sc[u["slot"], at, :] * factor - u["m2"])
        s_sc[u["slot"], at, :] = p
        part = fold(p, jnp.sum)
        u["l"] = part if u["l"] is None else u["l"] + part
        o = dot(vt_sc[:, base(u, t) : base(u, t) + ROWS], p.astype(BF))
        u["o"] = o if u["o"] is None else u["o"] + o

    def close_weights(u):
        u["inv"] = 1.0 / jnp.sum(u["l"], axis=0, keepdims=True)
        attended = (u["o"] * u["inv"]).astype(BF).astype(F32)
        u["delta"] = jnp.sum(u["dt"].astype(F32) * attended, axis=0, keepdims=True)

    def grads(u, t):
        b, at = u["b"], slice(t * ROWS, (t + 1) * ROWS)
        keys = slice(base(u, t), base(u, t) + ROWS)
        dp = dot(v_sc[keys, :], u["dt"])
        p = s_sc[u["slot"], at, :] * u["inv"]
        ds = (p * (dp - u["delta"])).astype(BF)
        dk_sc[keys, :] += dot(ds, u["q"])
        dv_sc[keys, :] += dot(p.astype(BF), u["d"])
        dq = dot(kt_sc[:, keys], ds)
        u["dq"] = dq if u["dq"] is None else u["dq"] + dq

    def close_grads(u):
        rows = slice(u["b"] * ROWS, (u["b"] + 1) * ROWS)
        cols = slice(u["h"] * HEAD, (u["h"] + 1) * HEAD)
        dq_sc[rows, cols] = (u["dq"] * SCALE).T.astype(BF)

    for step in range(len(units) + 2):
        now, before, earlier = step < 8, 0 <= step - 1 < 8, 0 <= step - 2 < 8
        if now:
            open_unit(units[step])
        for t in range(6):
            if earlier:
                grads(units[step - 2], t)
            if before:
                weights(units[step - 1], t)
            if now:
                scores(units[step], t)
        if now:
            close_scores(units[step])
        if before:
            close_weights(units[step - 1])
        if earlier:
            close_grads(units[step - 2])
    emit()
    for done in outs:
        done.wait()


def attend(g, *args):
    shape = jax.ShapeDtypeStruct
    return pl.pallas_call(
        functools.partial(attend_kernel, g),
        in_specs=[VM] + [ANY] * (7 + g),
        out_specs=[ANY] * 6,
        out_shape=[
            shape((ROWS, 512), BF),
            shape((ROWS, 512), BF),
            shape((1024, HEAD), F32),
            shape((512, 256), F32),
            shape((512, 256), BF),
            shape((512, 256), BF),
        ],
        scratch_shapes=[
            pltpu.VMEM((SPAN, HEAD), BF),
            pltpu.VMEM((SPAN, HEAD), BF),
            pltpu.VMEM((HEAD, SPAN), BF),
            pltpu.VMEM((HEAD, SPAN), BF),
            pltpu.VMEM((3, 1536, ROWS), F32),
            pltpu.VMEM((512, 512), BF),
            pltpu.VMEM((512, 512), BF),
            pltpu.VMEM((512, 512), BF),
            pltpu.VMEM((SPAN, HEAD), F32),
            pltpu.VMEM((SPAN, HEAD), F32),
            pltpu.VMEM((3, ROWS, ROWS), F32),
            pltpu.VMEM((2, ROWS, ROWS), F32),
            pltpu.VMEM((512, 256), F32),
            pltpu.VMEM((2, 512, 256), BF),
            pltpu.VMEM((1024, HEAD), F32),
            pltpu.SemaphoreType.DMA((22,)),
            pltpu.SemaphoreType.DMA((8,)),
        ],
        compiler_params=pltpu.CompilerParams(vmem_limit_bytes=60 << 20),
        cost_estimate=pl.CostEstimate(
            flops=5_000_000_000, bytes_accessed=4_000_000, transcendentals=3_000_000
        ),
        name="attend",
    )(*args)


def gather_kernel(*refs):
    parts = (refs[:3], refs[3:6])
    dq_parts, mine_ref, theirs, dq_ref = refs[6:10], refs[10], refs[11:13], refs[13]
    core = place()[2]
    for g, (own, back1, back2) in enumerate(parts):
        total = own[...] + back1[...].astype(F32) + back2[...].astype(F32)
        mine_ref[:, g * 256 : (g + 1) * 256] = total[:ROWS]
        theirs[g][...] = total[ROWS:].astype(BF)
    for i, ref in enumerate(dq_parts):
        which = core if i % 2 == 0 else 1 - core
        dq_ref[:, window((2 * which + i // 2) * 512, 512)] = ref[...]


def gather(*args):
    shape = jax.ShapeDtypeStruct
    return pl.pallas_call(
        gather_kernel,
        in_specs=[VM] * 10,
        out_specs=[VM] * 4,
        out_shape=[
            shape((ROWS, 512), F32),
            shape((ROWS, 256), BF),
            shape((ROWS, 256), BF),
            shape((ROWS, 2048), BF),
        ],
        compiler_params=pltpu.CompilerParams(vmem_limit_bytes=60 << 20),
        cost_estimate=pl.CostEstimate(flops=GATHER_FLOPS, bytes_accessed=6_000_000, transcendentals=0),
        name="gather",
    )(*args)


def finish_kernel(pos_ref, mine_ref, recv0_ref, recv1_ref, share_ref, dk_ref, dv_ref):
    index, _, core = place()
    row = lax.broadcasted_iota(jnp.int32, (ROWS, HEAD), 0)
    first = pos_ref[2 * index] - index * ROWS
    second = pos_ref[2 * index + 1] - index * ROWS
    shares = []
    for source in range(2):
        share = share_ref[source]
        for i in range(1, share_ref.shape[0] // 2):
            share = share + share_ref[2 * i + source]
        shares.append(share)
    for half in range(2):
        which = core if half == 0 else 1 - core
        share = jnp.where(which == 0, shares[0], shares[1])
        for g in range(2):
            for i, out in enumerate((dk_ref, dv_ref)):
                at = 4 * g + 2 * i
                if half == 0:
                    total = mine_ref[:, (2 * g + i) * HEAD : (2 * g + i + 1) * HEAD]
                else:
                    total = (recv0_ref, recv1_ref)[g][:, i * HEAD : (i + 1) * HEAD].astype(F32)
                total = total + jnp.where(row == first, share[at : at + 1], 0.0)
                total = total + jnp.where(row == second, share[at + 1 : at + 2], 0.0)
                out[:, window((2 * which + g) * HEAD, HEAD)] = total.astype(BF)


def finish(*args):
    shape = jax.ShapeDtypeStruct
    return pl.pallas_call(
        finish_kernel,
        in_specs=[SM] + [VM] * 4,
        out_specs=[VM, VM],
        out_shape=[shape((ROWS, 512), BF), shape((ROWS, 512), BF)],
        compiler_params=pltpu.CompilerParams(vmem_limit_bytes=60 << 20),
        name="finish",
    )(*args)


def to_sibling(block):
    return lax.ppermute(block, "ctx", [(i, i ^ 1) for i in range(lax.axis_size("ctx"))])


def to_chip(block, hops, flip=0):
    size = lax.axis_size("ctx")
    return lax.ppermute(block, "ctx", [(i, ((i + 2 * hops) % size) ^ flip) for i in range(size)])


def exchange(block):
    return lax.all_to_all(block, "ctx", 0, 0, tiled=True)


def body(queries, keys, values, cotangent, summary_positions):
    kv_own, kv_send, blocks, qd_send = pack(summary_positions, keys, values, queries, cotangent)
    kv_recv = to_sibling(kv_send)
    qd = to_sibling(qd_send)
    summ = exchange(blocks).reshape(1024, HEAD)
    kv0 = [jnp.concatenate([kv_own[g], kv_recv[g]], 0) for g in range(2)]
    kv1 = [to_chip(kv0[g], 1) for g in range(2)]
    kv2 = [to_chip(kv0[g], 2) for g in range(2)]
    sk0, sk1, pos = unpack(summary_positions.reshape(2, 128), summ)
    outs = attend(0, pos, queries, cotangent, qd, kv2[0], kv1[0], kv0[0], sk0)
    dq0, dqs0, summ_grad, own0, back1, back2 = outs
    back1_0, back2_0 = to_chip(back1, -1), to_chip(back2, -2)
    outs = attend(1, pos, queries, cotangent, qd, kv2[1], kv1[1], kv0[1], sk1, summ_grad)
    outs, back1_0, back2_0, dqs0 = lax.optimization_barrier((outs, back1_0, back2_0, dqs0))
    dq1, dqs1, summ_grad, own1, back1, back2 = outs
    back1_1, back2_1 = to_chip(back1, -1), to_chip(back2, -2)
    mine, theirs0, theirs1, query_grad = gather(
        own0, back1_0, back2_0, own1, back1_1, back2_1, dq0, to_sibling(dqs0), dq1, to_sibling(dqs1)
    )
    shares = exchange(summ_grad.reshape(128, 8, HEAD))
    key_grad, value_gradient = finish(
        summary_positions, mine, to_sibling(theirs0), to_sibling(theirs1), shares
    )
    return query_grad, key_grad, value_gradient


def solution(mesh):
    return jax.shard_map(
        body,
        mesh=mesh,
        in_specs=(P("ctx", None), P("ctx", None), P("ctx", None), P("ctx", None), P()),
        out_specs=(P("ctx", None), P("ctx", None), P("ctx", None)),
        check_vma=False,
    )
```

```python
import functools

import jax
import jax.numpy as jnp
from jax import lax
from jax.experimental import pallas as pl
from jax.experimental.pallas import tpu as pltpu
from jax.sharding import PartitionSpec as P

HEAD = 128
ROWS = 256
SPAN = 1792
GATHER_FLOPS = 6_000_000_000
UNPACK_FLOPS = 40_000_000_000
BIG = 3e38
NEG = -1e30
SCALE = HEAD**-0.5
LOG2E = 1.4426950408889634
F32 = jnp.float32
BF = jnp.bfloat16
VM = pl.BlockSpec(memory_space=pltpu.VMEM)
SM = pl.BlockSpec(memory_space=pltpu.SMEM)
HBM = pl.BlockSpec(memory_space=pltpu.HBM)
ANY = pl.BlockSpec(memory_space=pl.ANY)


def dot(a, b):
    return jnp.dot(a, b, preferred_element_type=F32)


def place():
    index = lax.axis_index("ctx")
    return index, index // 2, index % 2


def window(start, size):
    return pl.ds(pl.multiple_of(start, size), size)


def run(copies):
    for copy in copies:
        copy.start()
    for copy in copies:
        copy.wait()


def pack_kernel(pos_ref, k_ref, v_ref, q_hbm, d_hbm, own_ref, send_ref, block_ref, qd_ref, sem):
    index, _, core = place()
    copies = []
    for i, ref in enumerate((q_hbm, d_hbm)):
        src = ref.at[:, window((1 - core) * 1024, 1024)]
        copies.append(pltpu.make_async_copy(src, qd_ref.at[:, i * 1024 : (i + 1) * 1024], sem.at[i]))
        copies[-1].start()
    for out, which in ((own_ref, core), (send_ref, 1 - core)):
        for g in range(2):
            cols = window((2 * which + g) * HEAD, HEAD)
            out[g, :, :HEAD] = k_ref[:, cols]
            out[g, :, HEAD:] = v_ref[:, cols]
    slot = lax.broadcasted_iota(jnp.int32, (8, ROWS), 0)
    row = lax.broadcasted_iota(jnp.int32, (8, ROWS), 1)
    first = pos_ref[2 * index] - index * ROWS
    second = pos_ref[2 * index + 1] - index * ROWS
    wanted = jnp.where(slot % 2 == 0, first, second)
    tiles = []
    for which in range(2):
        tile = jnp.zeros((8, HEAD), F32)
        for g in range(2):
            for i, ref in enumerate((k_ref, v_ref)):
                pick = ((row == wanted) & (slot // 2 == 2 * g + i)).astype(F32).astype(BF)
                head = 2 * which + g
                tile = tile + dot(pick, ref[:, head * HEAD : (head + 1) * HEAD])
        tiles.append(tile.astype(BF))
    for device in range(block_ref.shape[0]):
        block_ref[device] = tiles[device % 2]
    for copy in copies:
        copy.wait()


def pack(pos, keys, values, queries, cotangent):
    shape = jax.ShapeDtypeStruct
    return pl.pallas_call(
        pack_kernel,
        in_specs=[SM, VM, VM, HBM, HBM],
        out_specs=[VM] * 4,
        out_shape=[
            shape((2, ROWS, 2 * HEAD), BF),
            shape((2, ROWS, 2 * HEAD), BF),
            shape((128, 8, HEAD), BF),
            shape((ROWS, 2048), BF),
        ],
        scratch_shapes=[pltpu.SemaphoreType.DMA((2,))],
        compiler_params=pltpu.CompilerParams(vmem_limit_bytes=60 << 20),
        name="pack",
    )(pos, keys, values, queries, cotangent)


def unpack_kernel(pos_ref, summ_ref, sk0_ref, sk1_ref, posb_ref, f_sc, t_sc):
    f_sc[...] = summ_ref[...].astype(F32)
    for g, out in enumerate((sk0_ref, sk1_ref)):
        for i in range(2):
            for r in range(2):
                slots = pl.ds(4 * g + 2 * i + r, 128, stride=8)
                t_sc[pl.ds(r, 128, stride=2), :] = f_sc[slots, :]
            out[:, i * HEAD : (i + 1) * HEAD] = t_sc[...].astype(BF)
    for i in range(2):
        row = jnp.broadcast_to(pos_ref[i : i + 1, :].astype(F32), (HEAD, HEAD))
        posb_ref[i * HEAD : (i + 1) * HEAD, :] = row.T


def unpack(pos, summ):
    shape = jax.ShapeDtypeStruct
    return pl.pallas_call(
        unpack_kernel,
        in_specs=[VM, VM],
        out_specs=[VM] * 3,
        out_shape=[shape((ROWS, 256), BF), shape((ROWS, 256), BF), shape((ROWS, HEAD), F32)],
        scratch_shapes=[pltpu.VMEM((1024, HEAD), F32), pltpu.VMEM((ROWS, HEAD), F32)],
        compiler_params=pltpu.CompilerParams(vmem_limit_bytes=16 << 20),
        cost_estimate=pl.CostEstimate(flops=UNPACK_FLOPS, bytes_accessed=1_000_000, transcendentals=0),
        name="unpack",
    )(pos, summ)


def fold(x, op):
    return op(x.reshape(x.shape[0] // 8, 8, x.shape[1]), axis=0)


def attend_kernel(g, pos_ref, q_hbm, d_hbm, qd_hbm, kv2, kv1, kv0, summ, *rest):
    before, rest = (rest[0], rest[1:]) if g else (None, rest)
    dqo_hbm, dqs_hbm, gs_hbm, grad_hbm = rest[0], rest[1], rest[2], rest[3:6]
    (k_sc, v_sc, kt_sc, vt_sc, s_sc, q_sc, d_sc, dq_sc, dk_sc, dv_sc, lim_sc, lims_sc) = rest[6:18]
    own_sc, bf_sc, gs_sc, sem, out_sem = rest[18:]
    _, chip, core = place()
    mine = window(core * ROWS, ROWS)
    theirs = window((1 - core) * ROWS, ROWS)
    copies = []

    def copy(src, dst):
        copies.append(pltpu.make_async_copy(src, dst, sem.at[len(copies)]))
        copies[-1].start()

    if g:
        copy(before, gs_sc)
    copy(q_hbm.at[:, window(core * 1024 + g * 512, 512)], q_sc.at[mine])
    copy(d_hbm.at[:, window(core * 1024 + g * 512, 512)], d_sc.at[mine])
    copy(qd_hbm.at[:, g * 512 : (g + 1) * 512], q_sc.at[theirs])
    copy(qd_hbm.at[:, 1024 + g * 512 : 1536 + g * 512], d_sc.at[theirs])
    for i, kv in enumerate((kv2, kv1, kv0)):
        for part in range(2):
            at = window(i * 512 + (core if part == 0 else 1 - core) * ROWS, ROWS)
            rows = slice(part * ROWS, (part + 1) * ROWS)
            copy(kv.at[rows, :HEAD], k_sc.at[at])
            copy(kv.at[rows, HEAD:], v_sc.at[at])
    copy(summ.at[:, :HEAD], k_sc.at[1536:])
    copy(summ.at[:, HEAD:], v_sc.at[1536:])
    ki = lax.broadcasted_iota(jnp.int32, (ROWS, ROWS), 0)
    qi = lax.broadcasted_iota(jnp.int32, (ROWS, ROWS), 1)
    pos = jnp.concatenate([pos_ref[...], pos_ref[...]], 1)
    for b in range(2):
        lim_sc[b] = jnp.where((ki > qi) & (chip * 2 + b >= 4), BIG, NEG)
        lims_sc[b] = jnp.where(pos <= ((chip * 2 + b) * ROWS + qi).astype(F32), BIG, NEG)
    lim_sc[2] = jnp.where(ki <= qi, BIG, NEG)
    dk_sc[...] = jnp.zeros_like(dk_sc)
    dv_sc[...] = jnp.zeros_like(dv_sc)
    for done in copies:
        done.wait()
    for i in range(7):
        at = slice(i * ROWS, (i + 1) * ROWS)
        kt_sc[:, at] = k_sc[at, :].T
        vt_sc[:, at] = v_sc[at, :].T
    outs = []

    def send(src, dst):
        outs.append(pltpu.make_async_copy(src, dst, out_sem.at[len(outs)]))
        outs[-1].start()

    def emit():
        send(dq_sc.at[mine], dqo_hbm)
        send(dq_sc.at[theirs], dqs_hbm)
        dk_sc[1536:, :] = dk_sc[1536:, :] * SCALE
        for i, acc in enumerate((dk_sc, dv_sc)):
            for r in range(2):
                slots = pl.ds(4 * g + 2 * i + r, 128, stride=8)
                gs_sc[slots, :] = acc[pl.ds(1536 + r, 128, stride=2), :]
        send(gs_sc, gs_hbm)
        for i, hbm in enumerate(grad_hbm):
            for part in range(2):
                at = window((2 - i) * 512 + (core if part == 0 else 1 - core) * ROWS, ROWS)
                rows = slice(part * ROWS, (part + 1) * ROWS)
                stage, kind = (own_sc, F32) if i == 0 else (bf_sc.at[i - 1], BF)
                stage[rows, :HEAD] = (dk_sc[at, :] * SCALE).astype(kind)
                stage[rows, HEAD:] = dv_sc[at, :].astype(kind)
            send(stage, hbm)

    factor = SCALE * LOG2E

    def base(u, t):
        return 1536 if t == 5 else (u["b"] + t) * ROWS

    units = [dict(b=u // 4, h=u % 4, slot=u % 3) for u in range(8)]

    def open_unit(u):
        rows = slice(u["b"] * ROWS, (u["b"] + 1) * ROWS)
        cols = slice(u["h"] * HEAD, (u["h"] + 1) * HEAD)
        u["q"], u["d"] = q_sc[rows, cols], d_sc[rows, cols]
        u["qt"], u["dt"] = u["q"].T, u["d"].T
        u["m"] = u["l"] = u["o"] = u["dq"] = None

    def scores(u, t):
        b, at = u["b"], slice(t * ROWS, (t + 1) * ROWS)
        s = dot(k_sc[base(u, t) : base(u, t) + ROWS, :], u["qt"])
        if t == 0:
            limit = lim_sc[b]
        elif t == 4:
            limit = lim_sc[2]
        elif t == 5:
            limit = lims_sc[b]
        else:
            limit = jnp.where(chip * 2 + b + t >= 4, BIG, NEG)
        s = jnp.minimum(s, limit)
        s_sc[u["slot"], at, :] = s
        m = fold(s, jnp.max)
        u["m"] = m if u["m"] is None else jnp.maximum(u["m"], m)

    def close_scores(u):
        u["m2"] = jnp.max(u["m"], axis=0, keepdims=True) * factor

    def weights(u, t):
        b, at = u["b"], slice(t * ROWS, (t + 1) * ROWS)
        p = jnp.exp2(s_sc[u["slot"], at, :] * factor - u["m2"])
        s_sc[u["slot"], at, :] = p
        part = fold(p, jnp.sum)
        u["l"] = part if u["l"] is None else u["l"] + part
        o = dot(vt_sc[:, base(u, t) : base(u, t) + ROWS], p.astype(BF))
        u["o"] = o if u["o"] is None else u["o"] + o

    def close_weights(u):
        u["inv"] = 1.0 / jnp.sum(u["l"], axis=0, keepdims=True)
        attended = (u["o"] * u["inv"]).astype(BF).astype(F32)
        u["delta"] = jnp.sum(u["dt"].astype(F32) * attended, axis=0, keepdims=True)

    def grads(u, t):
        b, at = u["b"], slice(t * ROWS, (t + 1) * ROWS)
        keys = slice(base(u, t), base(u, t) + ROWS)
        dp = dot(v_sc[keys, :], u["dt"])
        p = s_sc[u["slot"], at, :] * u["inv"]
        ds = (p * (dp - u["delta"])).astype(BF)
        dk_sc[keys, :] += dot(ds, u["q"])
        dv_sc[keys, :] += dot(p.astype(BF), u["d"])
        dq = dot(kt_sc[:, keys], ds)
        u["dq"] = dq if u["dq"] is None else u["dq"] + dq

    def close_grads(u):
        rows = slice(u["b"] * ROWS, (u["b"] + 1) * ROWS)
        cols = slice(u["h"] * HEAD, (u["h"] + 1) * HEAD)
        dq_sc[rows, cols] = (u["dq"] * SCALE).T.astype(BF)

    for step in range(len(units) + 2):
        now, before, earlier = step < 8, 0 <= step - 1 < 8, 0 <= step - 2 < 8
        if now:
            open_unit(units[step])
        for t in range(6):
            if earlier:
                grads(units[step - 2], t)
            if before:
                weights(units[step - 1], t)
            if now:
                scores(units[step], t)
        if now:
            close_scores(units[step])
        if before:
            close_weights(units[step - 1])
        if earlier:
            close_grads(units[step - 2])
    emit()
    for done in outs:
        done.wait()


def attend(g, *args):
    shape = jax.ShapeDtypeStruct
    return pl.pallas_call(
        functools.partial(attend_kernel, g),
        in_specs=[VM, HBM, HBM] + [ANY] * (5 + g),
        out_specs=[HBM] * 6,
        out_shape=[
            shape((ROWS, 512), BF),
            shape((ROWS, 512), BF),
            shape((1024, HEAD), F32),
            shape((512, 256), F32),
            shape((512, 256), BF),
            shape((512, 256), BF),
        ],
        scratch_shapes=[
            pltpu.VMEM((SPAN, HEAD), BF),
            pltpu.VMEM((SPAN, HEAD), BF),
            pltpu.VMEM((HEAD, SPAN), BF),
            pltpu.VMEM((HEAD, SPAN), BF),
            pltpu.VMEM((3, 1536, ROWS), F32),
            pltpu.VMEM((512, 512), BF),
            pltpu.VMEM((512, 512), BF),
            pltpu.VMEM((512, 512), BF),
            pltpu.VMEM((SPAN, HEAD), F32),
            pltpu.VMEM((SPAN, HEAD), F32),
            pltpu.VMEM((3, ROWS, ROWS), F32),
            pltpu.VMEM((2, ROWS, ROWS), F32),
            pltpu.VMEM((512, 256), F32),
            pltpu.VMEM((2, 512, 256), BF),
            pltpu.VMEM((1024, HEAD), F32),
            pltpu.SemaphoreType.DMA((22,)),
            pltpu.SemaphoreType.DMA((8,)),
        ],
        compiler_params=pltpu.CompilerParams(vmem_limit_bytes=24 << 20),
        cost_estimate=pl.CostEstimate(
            flops=5_000_000_000, bytes_accessed=4_000_000, transcendentals=3_000_000
        ),
        name="attend",
    )(*args)


def gather_kernel(*refs):
    parts = (refs[:3], refs[3:6])
    dq_parts, mine_ref, theirs, dq_ref = refs[6:10], refs[10], refs[11:13], refs[13]
    core = place()[2]
    for g, (own, back1, back2) in enumerate(parts):
        total = own[...] + back1[...].astype(F32) + back2[...].astype(F32)
        mine_ref[:, g * 256 : (g + 1) * 256] = total[:ROWS]
        theirs[g][...] = total[ROWS:].astype(BF)
    for i, ref in enumerate(dq_parts):
        which = core if i % 2 == 0 else 1 - core
        dq_ref[:, window((2 * which + i // 2) * 512, 512)] = ref[...]


def gather(*args):
    shape = jax.ShapeDtypeStruct
    return pl.pallas_call(
        gather_kernel,
        in_specs=[VM] * 10,
        out_specs=[VM] * 4,
        out_shape=[
            shape((ROWS, 512), F32),
            shape((ROWS, 256), BF),
            shape((ROWS, 256), BF),
            shape((ROWS, 2048), BF),
        ],
        compiler_params=pltpu.CompilerParams(vmem_limit_bytes=16 << 20),
        cost_estimate=pl.CostEstimate(flops=GATHER_FLOPS, bytes_accessed=6_000_000, transcendentals=0),
        name="gather",
    )(*args)


def finish_kernel(pos_ref, mine_ref, recv0_ref, recv1_ref, share_ref, dk_ref, dv_ref):
    index, _, core = place()
    row = lax.broadcasted_iota(jnp.int32, (ROWS, HEAD), 0)
    first = pos_ref[2 * index] - index * ROWS
    second = pos_ref[2 * index + 1] - index * ROWS
    shares = []
    for source in range(2):
        share = share_ref[source]
        for i in range(1, share_ref.shape[0] // 2):
            share = share + share_ref[2 * i + source]
        shares.append(share)
    for half in range(2):
        which = core if half == 0 else 1 - core
        share = jnp.where(which == 0, shares[0], shares[1])
        for g in range(2):
            for i, out in enumerate((dk_ref, dv_ref)):
                at = 4 * g + 2 * i
                if half == 0:
                    total = mine_ref[:, (2 * g + i) * HEAD : (2 * g + i + 1) * HEAD]
                else:
                    total = (recv0_ref, recv1_ref)[g][:, i * HEAD : (i + 1) * HEAD].astype(F32)
                total = total + jnp.where(row == first, share[at : at + 1], 0.0)
                total = total + jnp.where(row == second, share[at + 1 : at + 2], 0.0)
                out[:, window((2 * which + g) * HEAD, HEAD)] = total.astype(BF)


def finish(*args):
    shape = jax.ShapeDtypeStruct
    return pl.pallas_call(
        finish_kernel,
        in_specs=[SM] + [VM] * 4,
        out_specs=[VM, VM],
        out_shape=[shape((ROWS, 512), BF), shape((ROWS, 512), BF)],
        compiler_params=pltpu.CompilerParams(vmem_limit_bytes=16 << 20),
        name="finish",
    )(*args)


def to_sibling(block):
    return lax.ppermute(block, "ctx", [(i, i ^ 1) for i in range(lax.axis_size("ctx"))])


def to_chip(block, hops, flip=0):
    size = lax.axis_size("ctx")
    return lax.ppermute(block, "ctx", [(i, ((i + 2 * hops) % size) ^ flip) for i in range(size)])


def exchange(block):
    return lax.all_to_all(block, "ctx", 0, 0, tiled=True)


def body(queries, keys, values, cotangent, summary_positions):
    kv_own, kv_send, blocks, qd_send = pack(summary_positions, keys, values, queries, cotangent)
    kv_recv = to_sibling(kv_send)
    qd = to_sibling(qd_send)
    summ = exchange(blocks).reshape(1024, HEAD)
    kv0 = [jnp.concatenate([kv_own[g], kv_recv[g]], 0) for g in range(2)]
    kv1 = [to_chip(kv0[g], 1) for g in range(2)]
    kv2 = [to_chip(kv0[g], 2) for g in range(2)]
    sk0, sk1, pos = unpack(summary_positions.reshape(2, 128), summ)
    outs = attend(0, pos, queries, cotangent, qd, kv2[0], kv1[0], kv0[0], sk0)
    dq0, dqs0, summ_grad, own0, back1, back2 = outs
    back1_0, back2_0 = to_chip(back1, -1), to_chip(back2, -2)
    outs = attend(1, pos, queries, cotangent, qd, kv2[1], kv1[1], kv0[1], sk1, summ_grad)
    outs, back1_0, back2_0, dqs0 = lax.optimization_barrier((outs, back1_0, back2_0, dqs0))
    dq1, dqs1, summ_grad, own1, back1, back2 = outs
    back1_1, back2_1 = to_chip(back1, -1), to_chip(back2, -2)
    mine, theirs0, theirs1, query_grad = gather(
        own0, back1_0, back2_0, own1, back1_1, back2_1, dq0, to_sibling(dqs0), dq1, to_sibling(dqs1)
    )
    shares = exchange(summ_grad.reshape(128, 8, HEAD))
    key_grad, value_gradient = finish(
        summary_positions, mine, to_sibling(theirs0), to_sibling(theirs1), shares
    )
    return query_grad, key_grad, value_gradient


def solution(mesh):
    return jax.shard_map(
        body,
        mesh=mesh,
        in_specs=(P("ctx", None), P("ctx", None), P("ctx", None), P("ctx", None), P()),
        out_specs=(P("ctx", None), P("ctx", None), P("ctx", None)),
        check_vma=False,
    )
```

```python
import functools

import jax
import jax.numpy as jnp
from jax import lax
from jax.experimental import pallas as pl
from jax.experimental.pallas import tpu as pltpu
from jax.sharding import PartitionSpec as P

HEAD = 128
ROWS = 256
SPAN = 1792
GATHER_FLOPS = 6_000_000_000
UNPACK_FLOPS = 40_000_000_000
BIG = 3e38
NEG = -1e30
SCALE = HEAD**-0.5
LOG2E = 1.4426950408889634
F32 = jnp.float32
BF = jnp.bfloat16
VM = pl.BlockSpec(memory_space=pltpu.VMEM)
SM = pl.BlockSpec(memory_space=pltpu.SMEM)
HBM = pl.BlockSpec(memory_space=pltpu.HBM)
ANY = pl.BlockSpec(memory_space=pl.ANY)


def dot(a, b):
    return jnp.dot(a, b, preferred_element_type=F32)


def place():
    index = lax.axis_index("ctx")
    return index, index // 2, index % 2


def window(start, size):
    return pl.ds(pl.multiple_of(start, size), size)


def run(copies):
    for copy in copies:
        copy.start()
    for copy in copies:
        copy.wait()


def pack_kernel(
    pos_ref, k_hbm, v_hbm, q_hbm, d_hbm, own_hbm, send_hbm, block_hbm, qd_hbm,
    k_ref, v_ref, own_ref, send_ref, block_ref, qd_ref, sem, out_sem,
):
    index, _, core = place()
    outs = []

    def send(src, dst):
        outs.append(pltpu.make_async_copy(src, dst, out_sem.at[len(outs)]))
        outs[-1].start()

    loads = [pltpu.make_async_copy(k_hbm, k_ref, sem.at[0]), pltpu.make_async_copy(v_hbm, v_ref, sem.at[1])]
    for i, ref in enumerate((q_hbm, d_hbm)):
        src = ref.at[:, window((1 - core) * 1024, 1024)]
        loads.append(pltpu.make_async_copy(src, qd_ref.at[i], sem.at[2 + i]))
    for load in loads:
        load.start()
    loads[0].wait()
    loads[1].wait()
    for out, hbm, which in ((send_ref, send_hbm, 1 - core), (own_ref, own_hbm, core)):
        for g in range(2):
            cols = window((2 * which + g) * HEAD, HEAD)
            out[g, :, :HEAD] = k_ref[:, cols]
            out[g, :, HEAD:] = v_ref[:, cols]
        send(out, hbm)
    slot = lax.broadcasted_iota(jnp.int32, (8, ROWS), 0)
    row = lax.broadcasted_iota(jnp.int32, (8, ROWS), 1)
    first = pos_ref[2 * index] - index * ROWS
    second = pos_ref[2 * index + 1] - index * ROWS
    wanted = jnp.where(slot % 2 == 0, first, second)
    tiles = []
    for which in range(2):
        tile = jnp.zeros((8, HEAD), F32)
        for g in range(2):
            for i, ref in enumerate((k_ref, v_ref)):
                pick = ((row == wanted) & (slot // 2 == 2 * g + i)).astype(F32).astype(BF)
                head = 2 * which + g
                tile = tile + dot(pick, ref[:, head * HEAD : (head + 1) * HEAD])
        tiles.append(tile.astype(BF))
    for device in range(block_ref.shape[0]):
        block_ref[device] = tiles[device % 2]
    send(block_ref, block_hbm)
    for i in range(2):
        loads[2 + i].wait()
        send(qd_ref.at[i], qd_hbm.at[:, i * 1024 : (i + 1) * 1024])
    for done in outs:
        done.wait()


def pack(pos, keys, values, queries, cotangent):
    shape = jax.ShapeDtypeStruct
    return pl.pallas_call(
        pack_kernel,
        in_specs=[SM, HBM, HBM, HBM, HBM],
        out_specs=[HBM] * 4,
        out_shape=[
            shape((2, ROWS, 2 * HEAD), BF),
            shape((2, ROWS, 2 * HEAD), BF),
            shape((128, 8, HEAD), BF),
            shape((ROWS, 2048), BF),
        ],
        scratch_shapes=[
            pltpu.VMEM((ROWS, 512), BF),
            pltpu.VMEM((ROWS, 512), BF),
            pltpu.VMEM((2, ROWS, 256), BF),
            pltpu.VMEM((2, ROWS, 256), BF),
            pltpu.VMEM((128, 8, HEAD), BF),
            pltpu.VMEM((2, ROWS, 1024), BF),
            pltpu.SemaphoreType.DMA((4,)),
            pltpu.SemaphoreType.DMA((5,)),
        ],
        compiler_params=pltpu.CompilerParams(vmem_limit_bytes=60 << 20),
        name="pack",
    )(pos, keys, values, queries, cotangent)


def unpack_kernel(pos_ref, summ_ref, sk0_ref, sk1_ref, posb_ref, f_sc, t_sc):
    f_sc[...] = summ_ref[...].astype(F32)
    for g, out in enumerate((sk0_ref, sk1_ref)):
        for i in range(2):
            for r in range(2):
                slots = pl.ds(4 * g + 2 * i + r, 128, stride=8)
                t_sc[pl.ds(r, 128, stride=2), :] = f_sc[slots, :]
            out[:, i * HEAD : (i + 1) * HEAD] = t_sc[...].astype(BF)
    for i in range(2):
        row = jnp.broadcast_to(pos_ref[i : i + 1, :].astype(F32), (HEAD, HEAD))
        posb_ref[i * HEAD : (i + 1) * HEAD, :] = row.T


def unpack(pos, summ):
    shape = jax.ShapeDtypeStruct
    return pl.pallas_call(
        unpack_kernel,
        in_specs=[VM, VM],
        out_specs=[VM] * 3,
        out_shape=[shape((ROWS, 256), BF), shape((ROWS, 256), BF), shape((ROWS, HEAD), F32)],
        scratch_shapes=[pltpu.VMEM((1024, HEAD), F32), pltpu.VMEM((ROWS, HEAD), F32)],
        compiler_params=pltpu.CompilerParams(vmem_limit_bytes=16 << 20),
        cost_estimate=pl.CostEstimate(flops=UNPACK_FLOPS, bytes_accessed=1_000_000, transcendentals=0),
        name="unpack",
    )(pos, summ)


def fold(x, op):
    return op(x.reshape(x.shape[0] // 8, 8, x.shape[1]), axis=0)


def attend_kernel(g, pos_ref, q_hbm, d_hbm, qd_hbm, kv2, kv1, kv0, summ, *rest):
    before, rest = (rest[:3], rest[3:]) if g else (None, rest)
    dqo_hbm, dqs_hbm, gs_hbm, grad_hbm = rest[0], rest[1], rest[2], rest[3:6]
    (k_sc, v_sc, kt_sc, vt_sc, s_sc, q_sc, d_sc, dq_sc, dk_sc, dv_sc, lim_sc, lims_sc) = rest[6:18]
    own_sc, bf_sc, gs_sc, gsb_sc, dq_before, sem, out_sem = rest[18:]
    _, chip, core = place()
    mine = window(core * ROWS, ROWS)
    theirs = window((1 - core) * ROWS, ROWS)
    copies = []

    def copy(src, dst):
        copies.append(pltpu.make_async_copy(src, dst, sem.at[len(copies)]))
        copies[-1].start()

    if g:
        copy(before[0], gs_sc)
        copy(before[1], own_sc.at[:, :256])
        copy(before[2], dq_before)
    copy(q_hbm.at[:, window(core * 1024 + g * 512, 512)], q_sc.at[mine])
    copy(d_hbm.at[:, window(core * 1024 + g * 512, 512)], d_sc.at[mine])
    copy(qd_hbm.at[:, g * 512 : (g + 1) * 512], q_sc.at[theirs])
    copy(qd_hbm.at[:, 1024 + g * 512 : 1536 + g * 512], d_sc.at[theirs])
    for i, kv in enumerate((kv2, kv1, kv0)):
        for part in range(2):
            at = window(i * 512 + (core if part == 0 else 1 - core) * ROWS, ROWS)
            rows = slice(part * ROWS, (part + 1) * ROWS)
            copy(kv.at[rows, :HEAD], k_sc.at[at])
            copy(kv.at[rows, HEAD:], v_sc.at[at])
    copy(summ.at[:, :HEAD], k_sc.at[1536:])
    copy(summ.at[:, HEAD:], v_sc.at[1536:])
    ki = lax.broadcasted_iota(jnp.int32, (ROWS, ROWS), 0)
    qi = lax.broadcasted_iota(jnp.int32, (ROWS, ROWS), 1)
    pos = jnp.concatenate([pos_ref[...], pos_ref[...]], 1)
    for b in range(2):
        lim_sc[b] = jnp.where((ki > qi) & (chip * 2 + b >= 4), BIG, NEG)
        lims_sc[b] = jnp.where(pos <= ((chip * 2 + b) * ROWS + qi).astype(F32), BIG, NEG)
    lim_sc[2] = jnp.where(ki <= qi, BIG, NEG)
    dk_sc[...] = jnp.zeros_like(dk_sc)
    dv_sc[...] = jnp.zeros_like(dv_sc)
    for done in copies:
        done.wait()
    for i in range(7):
        at = slice(i * ROWS, (i + 1) * ROWS)
        kt_sc[:, at] = k_sc[at, :].T
        vt_sc[:, at] = v_sc[at, :].T
    outs = []

    def send(src, dst):
        outs.append(pltpu.make_async_copy(src, dst, out_sem.at[len(outs)]))
        outs[-1].start()

    def emit():
        if g:
            send(dq_before, dqo_hbm.at[:, :512])
            send(dq_sc.at[mine], dqo_hbm.at[:, 512:])
        else:
            send(dq_sc.at[mine], dqo_hbm)
        send(dq_sc.at[theirs], dqs_hbm)
        dk_sc[1536:, :] = dk_sc[1536:, :] * SCALE
        for i, acc in enumerate((dk_sc, dv_sc)):
            for r in range(2):
                slots = pl.ds(4 * g + 2 * i + r, 128, stride=8)
                gs_sc[slots, :] = acc[pl.ds(1536 + r, 128, stride=2), :]
        if g:
            gsb_sc[...] = gs_sc[...].astype(BF)
        send(gsb_sc if g else gs_sc, gs_hbm)
        for i, hbm in enumerate(grad_hbm):
            for part in range(2):
                at = window((2 - i) * 512 + (core if part == 0 else 1 - core) * ROWS, ROWS)
                rows = slice(part * ROWS, (part + 1) * ROWS)
                stage, kind = (own_sc.at[:, g * 256 :], F32) if i == 0 else (bf_sc.at[i - 1], BF)
                stage[rows, :HEAD] = (dk_sc[at, :] * SCALE).astype(kind)
                stage[rows, HEAD:] = dv_sc[at, :].astype(kind)
            send(own_sc if i == 0 else stage, hbm)

    factor = SCALE * LOG2E

    def base(u, t):
        return 1536 if t == 5 else (u["b"] + t) * ROWS

    units = [dict(b=u // 4, h=u % 4, slot=u % 3) for u in range(8)]

    def open_unit(u):
        rows = slice(u["b"] * ROWS, (u["b"] + 1) * ROWS)
        cols = slice(u["h"] * HEAD, (u["h"] + 1) * HEAD)
        u["q"], u["d"] = q_sc[rows, cols], d_sc[rows, cols]
        u["qt"], u["dt"] = u["q"].T, u["d"].T
        u["m"] = u["l"] = u["o"] = u["dq"] = None

    def scores(u, t):
        b, at = u["b"], slice(t * ROWS, (t + 1) * ROWS)
        s = dot(k_sc[base(u, t) : base(u, t) + ROWS, :], u["qt"])
        if t == 0:
            limit = lim_sc[b]
        elif t == 4:
            limit = lim_sc[2]
        elif t == 5:
            limit = lims_sc[b]
        else:
            limit = jnp.where(chip * 2 + b + t >= 4, BIG, NEG)
        s = jnp.minimum(s, limit)
        s_sc[u["slot"], at, :] = s
        m = fold(s, jnp.max)
        u["m"] = m if u["m"] is None else jnp.maximum(u["m"], m)

    def close_scores(u):
        u["m2"] = jnp.max(u["m"], axis=0, keepdims=True) * factor

    def weights(u, t):
        b, at = u["b"], slice(t * ROWS, (t + 1) * ROWS)
        p = jnp.exp2(s_sc[u["slot"], at, :] * factor - u["m2"])
        s_sc[u["slot"], at, :] = p
        part = fold(p, jnp.sum)
        u["l"] = part if u["l"] is None else u["l"] + part
        o = dot(vt_sc[:, base(u, t) : base(u, t) + ROWS], p.astype(BF))
        u["o"] = o if u["o"] is None else u["o"] + o

    def close_weights(u):
        u["inv"] = 1.0 / jnp.sum(u["l"], axis=0, keepdims=True)
        attended = (u["o"] * u["inv"]).astype(BF).astype(F32)
        u["delta"] = jnp.sum(u["dt"].astype(F32) * attended, axis=0, keepdims=True)

    def grads(u, t):
        b, at = u["b"], slice(t * ROWS, (t + 1) * ROWS)
        keys = slice(base(u, t), base(u, t) + ROWS)
        dp = dot(v_sc[keys, :], u["dt"])
        p = s_sc[u["slot"], at, :] * u["inv"]
        ds = (p * (dp - u["delta"])).astype(BF)
        dk_sc[keys, :] += dot(ds, u["q"])
        dv_sc[keys, :] += dot(p.astype(BF), u["d"])
        dq = dot(kt_sc[:, keys], ds)
        u["dq"] = dq if u["dq"] is None else u["dq"] + dq

    def close_grads(u):
        rows = slice(u["b"] * ROWS, (u["b"] + 1) * ROWS)
        cols = slice(u["h"] * HEAD, (u["h"] + 1) * HEAD)
        dq_sc[rows, cols] = (u["dq"] * SCALE).T.astype(BF)

    for step in range(len(units) + 2):
        now, before, earlier = step < 8, 0 <= step - 1 < 8, 0 <= step - 2 < 8
        if now:
            open_unit(units[step])
        for t in range(6):
            if earlier:
                grads(units[step - 2], t)
            if before:
                weights(units[step - 1], t)
            if now:
                scores(units[step], t)
        if now:
            close_scores(units[step])
        if before:
            close_weights(units[step - 1])
        if earlier:
            close_grads(units[step - 2])
    emit()
    for done in outs:
        done.wait()


def attend(g, *args):
    shape = jax.ShapeDtypeStruct
    return pl.pallas_call(
        functools.partial(attend_kernel, g),
        in_specs=[VM, HBM, HBM] + [ANY] * (5 + 3 * g),
        out_specs=[HBM] * 6,
        out_shape=[
            shape((ROWS, 512 + 512 * g), BF),
            shape((ROWS, 512), BF),
            shape((1024, HEAD), BF if g else F32),
            shape((512, 256 + 256 * g), F32),
            shape((512, 256), BF),
            shape((512, 256), BF),
        ],
        scratch_shapes=[
            pltpu.VMEM((SPAN, HEAD), BF),
            pltpu.VMEM((SPAN, HEAD), BF),
            pltpu.VMEM((HEAD, SPAN), BF),
            pltpu.VMEM((HEAD, SPAN), BF),
            pltpu.VMEM((3, 1536, ROWS), F32),
            pltpu.VMEM((512, 512), BF),
            pltpu.VMEM((512, 512), BF),
            pltpu.VMEM((512, 512), BF),
            pltpu.VMEM((SPAN, HEAD), F32),
            pltpu.VMEM((SPAN, HEAD), F32),
            pltpu.VMEM((3, ROWS, ROWS), F32),
            pltpu.VMEM((2, ROWS, ROWS), F32),
            pltpu.VMEM((512, 256 + 256 * g), F32),
            pltpu.VMEM((2, 512, 256), BF),
            pltpu.VMEM((1024, HEAD), F32),
            pltpu.VMEM((1024, HEAD), BF),
            pltpu.VMEM((ROWS, 512), BF),
            pltpu.SemaphoreType.DMA((24,)),
            pltpu.SemaphoreType.DMA((8,)),
        ],
        compiler_params=pltpu.CompilerParams(vmem_limit_bytes=24 << 20),
        cost_estimate=pl.CostEstimate(
            flops=5_000_000_000, bytes_accessed=4_000_000, transcendentals=3_000_000
        ),
        name="attend",
    )(*args)


def gather_kernel(own, b10, b20, b11, b21, dq_own, dqr0, dqr1, mine_ref, their0, their1, dq_ref):
    core = place()[2]
    for g, (back1, back2, their) in enumerate(((b10, b20, their0), (b11, b21, their1))):
        cols = slice(g * 256, (g + 1) * 256)
        total = own[:, cols] + back1[...].astype(F32) + back2[...].astype(F32)
        mine_ref[:, cols] = total[:ROWS]
        their[...] = total[ROWS:].astype(BF)
        dq_ref[:, window(((1 - core) * 2 + g) * 512, 512)] = (dqr0, dqr1)[g][...]
    dq_ref[:, window(core * 1024, 1024)] = dq_own[...]


def gather(*args):
    shape = jax.ShapeDtypeStruct
    return pl.pallas_call(
        gather_kernel,
        in_specs=[VM] * 8,
        out_specs=[VM] * 4,
        out_shape=[
            shape((ROWS, 512), F32),
            shape((ROWS, 256), BF),
            shape((ROWS, 256), BF),
            shape((ROWS, 2048), BF),
        ],
        compiler_params=pltpu.CompilerParams(vmem_limit_bytes=16 << 20),
        cost_estimate=pl.CostEstimate(flops=GATHER_FLOPS, bytes_accessed=6_000_000, transcendentals=0),
        name="gather",
    )(*args)


def finish_kernel(pos_ref, mine_ref, recv0_ref, recv1_ref, share_ref, dk_ref, dv_ref):
    index, _, core = place()
    row = lax.broadcasted_iota(jnp.int32, (ROWS, HEAD), 0)
    first = pos_ref[2 * index] - index * ROWS
    second = pos_ref[2 * index + 1] - index * ROWS
    shares = []
    for source in range(2):
        share = share_ref[source].astype(F32)
        for i in range(1, share_ref.shape[0] // 2):
            share = share + share_ref[2 * i + source].astype(F32)
        shares.append(share)
    for half in range(2):
        which = core if half == 0 else 1 - core
        share = jnp.where(which == 0, shares[0], shares[1])
        for g in range(2):
            for i, out in enumerate((dk_ref, dv_ref)):
                at = 4 * g + 2 * i
                if half == 0:
                    total = mine_ref[:, (2 * g + i) * HEAD : (2 * g + i + 1) * HEAD]
                else:
                    total = (recv0_ref, recv1_ref)[g][:, i * HEAD : (i + 1) * HEAD].astype(F32)
                total = total + jnp.where(row == first, share[at : at + 1], 0.0)
                total = total + jnp.where(row == second, share[at + 1 : at + 2], 0.0)
                out[:, window((2 * which + g) * HEAD, HEAD)] = total.astype(BF)


def finish(*args):
    shape = jax.ShapeDtypeStruct
    return pl.pallas_call(
        finish_kernel,
        in_specs=[SM] + [VM] * 4,
        out_specs=[VM, VM],
        out_shape=[shape((ROWS, 512), BF), shape((ROWS, 512), BF)],
        compiler_params=pltpu.CompilerParams(vmem_limit_bytes=16 << 20),
        name="finish",
    )(*args)


def to_sibling(block):
    return lax.ppermute(block, "ctx", [(i, i ^ 1) for i in range(lax.axis_size("ctx"))])


def to_chip(block, hops, flip=0):
    size = lax.axis_size("ctx")
    return lax.ppermute(block, "ctx", [(i, ((i + 2 * hops) % size) ^ flip) for i in range(size)])


def exchange(block):
    return lax.all_to_all(block, "ctx", 0, 0, tiled=True)


def body(queries, keys, values, cotangent, summary_positions):
    kv_own, kv_send, blocks, qd_send = pack(summary_positions, keys, values, queries, cotangent)
    kv_recv = to_sibling(kv_send)
    qd = to_sibling(qd_send)
    summ = exchange(blocks).reshape(1024, HEAD)
    kv0 = [jnp.concatenate([kv_own[g], kv_recv[g]], 0) for g in range(2)]
    kv1 = [to_chip(kv0[g], 1) for g in range(2)]
    kv2 = [to_chip(kv0[g], 2) for g in range(2)]
    sk0, sk1, pos = unpack(summary_positions.reshape(2, 128), summ)
    outs = attend(0, pos, queries, cotangent, qd, kv2[0], kv1[0], kv0[0], sk0)
    dq0, dqs0, summ_grad, own0, back1, back2 = outs
    back1_0, back2_0 = to_chip(back1, -1), to_chip(back2, -2)
    outs = attend(1, pos, queries, cotangent, qd, kv2[1], kv1[1], kv0[1], sk1, summ_grad, own0, dq0)
    outs, back1_0, back2_0, dqs0 = lax.optimization_barrier((outs, back1_0, back2_0, dqs0))
    dq_own, dqs1, summ_grad, own, back1, back2 = outs
    back1_1, back2_1 = to_chip(back1, -1), to_chip(back2, -2)
    mine, theirs0, theirs1, query_grad = gather(
        own, back1_0, back2_0, back1_1, back2_1, dq_own, to_sibling(dqs0), to_sibling(dqs1)
    )
    shares = exchange(summ_grad.reshape(128, 8, HEAD))
    key_grad, value_gradient = finish(
        summary_positions, mine, to_sibling(theirs0), to_sibling(theirs1), shares
    )
    return query_grad, key_grad, value_gradient


def solution(mesh):
    return jax.shard_map(
        body,
        mesh=mesh,
        in_specs=(P("ctx", None), P("ctx", None), P("ctx", None), P("ctx", None), P()),
        out_specs=(P("ctx", None), P("ctx", None), P("ctx", None)),
        check_vma=False,
    )
```

```python
import functools

import jax
import jax.numpy as jnp
from jax import lax
from jax.experimental import pallas as pl
from jax.experimental.pallas import tpu as pltpu
from jax.sharding import PartitionSpec as P

HEAD = 128
ROWS = 256
SPAN = 1792
GATHER_FLOPS = 6_000_000_000
UNPACK_FLOPS = 40_000_000_000
BIG = 3e38
NEG = -1e30
SCALE = HEAD**-0.5
LOG2E = 1.4426950408889634
F32 = jnp.float32
BF = jnp.bfloat16
VM = pl.BlockSpec(memory_space=pltpu.VMEM)
SM = pl.BlockSpec(memory_space=pltpu.SMEM)
HBM = pl.BlockSpec(memory_space=pltpu.HBM)
ANY = pl.BlockSpec(memory_space=pl.ANY)


def dot(a, b):
    return jnp.dot(a, b, preferred_element_type=F32)


def place():
    index = lax.axis_index("ctx")
    return index, index // 2, index % 2


def window(start, size):
    return pl.ds(pl.multiple_of(start, size), size)


def run(copies):
    for copy in copies:
        copy.start()
    for copy in copies:
        copy.wait()


def pack_kernel(
    pos_ref, k_hbm, v_hbm, q_hbm, d_hbm, own_hbm, send_hbm, block_hbm, qd_hbm,
    k_ref, v_ref, own_ref, send_ref, block_ref, qd_ref, sem, out_sem,
):
    index, _, core = place()
    outs = []

    def send(src, dst):
        outs.append(pltpu.make_async_copy(src, dst, out_sem.at[len(outs)]))
        outs[-1].start()

    loads = [pltpu.make_async_copy(k_hbm, k_ref, sem.at[0]), pltpu.make_async_copy(v_hbm, v_ref, sem.at[1])]
    for i, ref in enumerate((q_hbm, d_hbm)):
        src = ref.at[:, window((1 - core) * 1024, 1024)]
        loads.append(pltpu.make_async_copy(src, qd_ref.at[i], sem.at[2 + i]))
    for load in loads:
        load.start()
    loads[0].wait()
    loads[1].wait()
    for out, hbm, which in ((send_ref, send_hbm, 1 - core), (own_ref, own_hbm, core)):
        for g in range(2):
            cols = window((2 * which + g) * HEAD, HEAD)
            out[g, :, :HEAD] = k_ref[:, cols]
            out[g, :, HEAD:] = v_ref[:, cols]
        send(out, hbm)
    slot = lax.broadcasted_iota(jnp.int32, (8, ROWS), 0)
    row = lax.broadcasted_iota(jnp.int32, (8, ROWS), 1)
    first = pos_ref[2 * index] - index * ROWS
    second = pos_ref[2 * index + 1] - index * ROWS
    wanted = jnp.where(slot % 2 == 0, first, second)
    tiles = []
    for which in range(2):
        tile = jnp.zeros((8, HEAD), F32)
        for g in range(2):
            for i, ref in enumerate((k_ref, v_ref)):
                pick = ((row == wanted) & (slot // 2 == 2 * g + i)).astype(F32).astype(BF)
                head = 2 * which + g
                tile = tile + dot(pick, ref[:, head * HEAD : (head + 1) * HEAD])
        tiles.append(tile.astype(BF))
    for device in range(block_ref.shape[0]):
        block_ref[device] = tiles[device % 2]
    send(block_ref, block_hbm)
    for i in range(2):
        loads[2 + i].wait()
        send(qd_ref.at[i], qd_hbm.at[:, i * 1024 : (i + 1) * 1024])
    for done in outs:
        done.wait()


def pack(pos, keys, values, queries, cotangent):
    shape = jax.ShapeDtypeStruct
    return pl.pallas_call(
        pack_kernel,
        in_specs=[SM, HBM, HBM, HBM, HBM],
        out_specs=[HBM] * 4,
        out_shape=[
            shape((2, ROWS, 2 * HEAD), BF),
            shape((2, ROWS, 2 * HEAD), BF),
            shape((128, 8, HEAD), BF),
            shape((ROWS, 2048), BF),
        ],
        scratch_shapes=[
            pltpu.VMEM((ROWS, 512), BF),
            pltpu.VMEM((ROWS, 512), BF),
            pltpu.VMEM((2, ROWS, 256), BF),
            pltpu.VMEM((2, ROWS, 256), BF),
            pltpu.VMEM((128, 8, HEAD), BF),
            pltpu.VMEM((2, ROWS, 1024), BF),
            pltpu.SemaphoreType.DMA((4,)),
            pltpu.SemaphoreType.DMA((5,)),
        ],
        compiler_params=pltpu.CompilerParams(vmem_limit_bytes=60 << 20),
        name="pack",
    )(pos, keys, values, queries, cotangent)


def unpack_kernel(pos_ref, summ_ref, sk0_ref, sk1_ref, posb_ref, f_sc, t_sc):
    f_sc[...] = summ_ref[...].astype(F32)
    for g, out in enumerate((sk0_ref, sk1_ref)):
        for i in range(2):
            for r in range(2):
                slots = pl.ds(4 * g + 2 * i + r, 128, stride=8)
                t_sc[pl.ds(r, 128, stride=2), :] = f_sc[slots, :]
            out[:, i * HEAD : (i + 1) * HEAD] = t_sc[...].astype(BF)
    for i in range(2):
        row = jnp.broadcast_to(pos_ref[i : i + 1, :].astype(F32), (HEAD, HEAD))
        posb_ref[i * HEAD : (i + 1) * HEAD, :] = row.T


def unpack(pos, summ):
    shape = jax.ShapeDtypeStruct
    return pl.pallas_call(
        unpack_kernel,
        in_specs=[VM, VM],
        out_specs=[VM] * 3,
        out_shape=[shape((ROWS, 256), BF), shape((ROWS, 256), BF), shape((ROWS, HEAD), F32)],
        scratch_shapes=[pltpu.VMEM((1024, HEAD), F32), pltpu.VMEM((ROWS, HEAD), F32)],
        compiler_params=pltpu.CompilerParams(vmem_limit_bytes=16 << 20),
        cost_estimate=pl.CostEstimate(flops=UNPACK_FLOPS, bytes_accessed=1_000_000, transcendentals=0),
        name="unpack",
    )(pos, summ)


def fold(x, op):
    return op(x.reshape(x.shape[0] // 8, 8, x.shape[1]), axis=0)


def attend_kernel(g, pos_ref, q_hbm, d_hbm, qd_hbm, kv2, kv1, kv0, summ, *rest):
    before, rest = (rest[:3], rest[3:]) if g else (None, rest)
    dqo_hbm, dqs_hbm, gs_hbm, grad_hbm = rest[0], rest[1], rest[2], rest[3:6]
    (k_sc, v_sc, kt_sc, vt_sc, s_sc, q_sc, d_sc, dq_sc, dk_sc, dv_sc, lim_sc, lims_sc) = rest[6:18]
    own_sc, bf_sc, gs_sc, gsb_sc, dq_before, sem, out_sem = rest[18:]
    _, chip, core = place()
    mine = window(core * ROWS, ROWS)
    theirs = window((1 - core) * ROWS, ROWS)
    copies = []

    def copy(src, dst):
        copies.append(pltpu.make_async_copy(src, dst, sem.at[len(copies)]))
        copies[-1].start()

    if g:
        copy(before[0], gs_sc)
        copy(before[1], own_sc.at[:, :256])
        copy(before[2], dq_before)
    copy(q_hbm.at[:, window(core * 1024 + g * 512, 512)], q_sc.at[mine])
    copy(d_hbm.at[:, window(core * 1024 + g * 512, 512)], d_sc.at[mine])
    copy(qd_hbm.at[:, g * 512 : (g + 1) * 512], q_sc.at[theirs])
    copy(qd_hbm.at[:, 1024 + g * 512 : 1536 + g * 512], d_sc.at[theirs])
    for i, kv in enumerate((kv2, kv1, kv0)):
        for part in range(2):
            at = window(i * 512 + (core if part == 0 else 1 - core) * ROWS, ROWS)
            rows = slice(part * ROWS, (part + 1) * ROWS)
            copy(kv.at[rows, :HEAD], k_sc.at[at])
            copy(kv.at[rows, HEAD:], v_sc.at[at])
    copy(summ.at[:, :HEAD], k_sc.at[1536:])
    copy(summ.at[:, HEAD:], v_sc.at[1536:])
    ki = lax.broadcasted_iota(jnp.int32, (ROWS, ROWS), 0)
    qi = lax.broadcasted_iota(jnp.int32, (ROWS, ROWS), 1)
    pos = jnp.concatenate([pos_ref[...], pos_ref[...]], 1)
    for b in range(2):
        lim_sc[b] = jnp.where((ki > qi) & (chip * 2 + b >= 4), BIG, NEG)
        lims_sc[b] = jnp.where(pos <= ((chip * 2 + b) * ROWS + qi).astype(F32), BIG, NEG)
    lim_sc[2] = jnp.where(ki <= qi, BIG, NEG)
    for done in copies:
        done.wait()
    for i in range(7):
        at = slice(i * ROWS, (i + 1) * ROWS)
        kt_sc[:, at] = k_sc[at, :].T
        vt_sc[:, at] = v_sc[at, :].T
    outs = []

    def send(src, dst):
        outs.append(pltpu.make_async_copy(src, dst, out_sem.at[len(outs)]))
        outs[-1].start()

    def emit():
        if g:
            send(dq_before, dqo_hbm.at[:, :512])
            send(dq_sc.at[mine], dqo_hbm.at[:, 512:])
        else:
            send(dq_sc.at[mine], dqo_hbm)
        send(dq_sc.at[theirs], dqs_hbm)
        dk_sc[1536:, :] = dk_sc[1536:, :] * SCALE
        for i, acc in enumerate((dk_sc, dv_sc)):
            for r in range(2):
                slots = pl.ds(4 * g + 2 * i + r, 128, stride=8)
                gs_sc[slots, :] = acc[pl.ds(1536 + r, 128, stride=2), :]
        if g:
            gsb_sc[...] = gs_sc[...].astype(BF)
        send(gsb_sc if g else gs_sc, gs_hbm)
        for i, hbm in enumerate(grad_hbm):
            for part in range(2):
                at = window((2 - i) * 512 + (core if part == 0 else 1 - core) * ROWS, ROWS)
                rows = slice(part * ROWS, (part + 1) * ROWS)
                stage, kind = (own_sc.at[:, g * 256 :], F32) if i == 0 else (bf_sc.at[i - 1], BF)
                stage[rows, :HEAD] = (dk_sc[at, :] * SCALE).astype(kind)
                stage[rows, HEAD:] = dv_sc[at, :].astype(kind)
            send(own_sc if i == 0 else stage, hbm)

    factor = SCALE * LOG2E

    def base(u, t):
        return 1536 if t == 5 else (u["b"] + t) * ROWS

    units = [dict(b=u // 4, h=u % 4, slot=u % 3) for u in range(8)]

    def open_unit(u):
        rows = slice(u["b"] * ROWS, (u["b"] + 1) * ROWS)
        cols = slice(u["h"] * HEAD, (u["h"] + 1) * HEAD)
        u["q"], u["d"] = q_sc[rows, cols], d_sc[rows, cols]
        u["qt"], u["dt"] = u["q"].T, u["d"].T
        u["m"] = u["l"] = u["o"] = u["dq"] = None

    def scores(u, t):
        b, at = u["b"], slice(t * ROWS, (t + 1) * ROWS)
        s = dot(k_sc[base(u, t) : base(u, t) + ROWS, :], u["qt"])
        if t == 0:
            limit = lim_sc[b]
        elif t == 4:
            limit = lim_sc[2]
        elif t == 5:
            limit = lims_sc[b]
        else:
            limit = jnp.where(chip * 2 + b + t >= 4, BIG, NEG)
        s = jnp.minimum(s, limit)
        s_sc[u["slot"], at, :] = s
        m = fold(s, jnp.max)
        u["m"] = m if u["m"] is None else jnp.maximum(u["m"], m)

    def close_scores(u):
        u["m2"] = jnp.max(u["m"], axis=0, keepdims=True) * factor

    def weights(u, t):
        b, at = u["b"], slice(t * ROWS, (t + 1) * ROWS)
        p = jnp.exp2(s_sc[u["slot"], at, :] * factor - u["m2"])
        s_sc[u["slot"], at, :] = p
        part = fold(p, jnp.sum)
        u["l"] = part if u["l"] is None else u["l"] + part
        o = dot(vt_sc[:, base(u, t) : base(u, t) + ROWS], p.astype(BF))
        u["o"] = o if u["o"] is None else u["o"] + o

    def close_weights(u):
        u["inv"] = 1.0 / jnp.sum(u["l"], axis=0, keepdims=True)
        attended = (u["o"] * u["inv"]).astype(BF).astype(F32)
        u["delta"] = jnp.sum(u["dt"].astype(F32) * attended, axis=0, keepdims=True)

    def grads(u, t):
        b, at = u["b"], slice(t * ROWS, (t + 1) * ROWS)
        keys = slice(base(u, t), base(u, t) + ROWS)
        dp = dot(v_sc[keys, :], u["dt"])
        p = s_sc[u["slot"], at, :] * u["inv"]
        ds = (p * (dp - u["delta"])).astype(BF)
        dk, dv = dot(ds, u["q"]), dot(p.astype(BF), u["d"])
        if u["h"] == 0 and (u["b"] == 0 or t == 4):
            dk_sc[keys, :] = dk
            dv_sc[keys, :] = dv
        else:
            dk_sc[keys, :] += dk
            dv_sc[keys, :] += dv
        dq = dot(kt_sc[:, keys], ds)
        u["dq"] = dq if u["dq"] is None else u["dq"] + dq

    def close_grads(u):
        rows = slice(u["b"] * ROWS, (u["b"] + 1) * ROWS)
        cols = slice(u["h"] * HEAD, (u["h"] + 1) * HEAD)
        dq_sc[rows, cols] = (u["dq"] * SCALE).T.astype(BF)

    for step in range(len(units) + 2):
        now, before, earlier = step < 8, 0 <= step - 1 < 8, 0 <= step - 2 < 8
        if now:
            open_unit(units[step])
        for t in range(6):
            if earlier:
                grads(units[step - 2], t)
            if before:
                weights(units[step - 1], t)
            if now:
                scores(units[step], t)
        if now:
            close_scores(units[step])
        if before:
            close_weights(units[step - 1])
        if earlier:
            close_grads(units[step - 2])
    emit()
    for done in outs:
        done.wait()


def attend(g, *args):
    shape = jax.ShapeDtypeStruct
    return pl.pallas_call(
        functools.partial(attend_kernel, g),
        in_specs=[VM, HBM, HBM] + [ANY] * (5 + 3 * g),
        out_specs=[HBM] * 6,
        out_shape=[
            shape((ROWS, 512 + 512 * g), BF),
            shape((ROWS, 512), BF),
            shape((1024, HEAD), BF if g else F32),
            shape((512, 256 + 256 * g), F32),
            shape((512, 256), BF),
            shape((512, 256), BF),
        ],
        scratch_shapes=[
            pltpu.VMEM((SPAN, HEAD), BF),
            pltpu.VMEM((SPAN, HEAD), BF),
            pltpu.VMEM((HEAD, SPAN), BF),
            pltpu.VMEM((HEAD, SPAN), BF),
            pltpu.VMEM((3, 1536, ROWS), F32),
            pltpu.VMEM((512, 512), BF),
            pltpu.VMEM((512, 512), BF),
            pltpu.VMEM((512, 512), BF),
            pltpu.VMEM((SPAN, HEAD), F32),
            pltpu.VMEM((SPAN, HEAD), F32),
            pltpu.VMEM((3, ROWS, ROWS), F32),
            pltpu.VMEM((2, ROWS, ROWS), F32),
            pltpu.VMEM((512, 256 + 256 * g), F32),
            pltpu.VMEM((2, 512, 256), BF),
            pltpu.VMEM((1024, HEAD), F32),
            pltpu.VMEM((1024, HEAD), BF),
            pltpu.VMEM((ROWS, 512), BF),
            pltpu.SemaphoreType.DMA((24,)),
            pltpu.SemaphoreType.DMA((8,)),
        ],
        compiler_params=pltpu.CompilerParams(vmem_limit_bytes=24 << 20),
        cost_estimate=pl.CostEstimate(
            flops=5_000_000_000, bytes_accessed=4_000_000, transcendentals=3_000_000
        ),
        name="attend",
    )(*args)


def gather_kernel(own, b10, b20, b11, b21, dq_own, dqr0, dqr1, mine_ref, their0, their1, dq_ref):
    core = place()[2]
    for g, (back1, back2, their) in enumerate(((b10, b20, their0), (b11, b21, their1))):
        cols = slice(g * 256, (g + 1) * 256)
        total = own[:, cols] + back1[...].astype(F32) + back2[...].astype(F32)
        mine_ref[:, cols] = total[:ROWS]
        their[...] = total[ROWS:].astype(BF)
        dq_ref[:, window(((1 - core) * 2 + g) * 512, 512)] = (dqr0, dqr1)[g][...]
    dq_ref[:, window(core * 1024, 1024)] = dq_own[...]


def gather(*args):
    shape = jax.ShapeDtypeStruct
    return pl.pallas_call(
        gather_kernel,
        in_specs=[VM] * 8,
        out_specs=[VM] * 4,
        out_shape=[
            shape((ROWS, 512), F32),
            shape((ROWS, 256), BF),
            shape((ROWS, 256), BF),
            shape((ROWS, 2048), BF),
        ],
        compiler_params=pltpu.CompilerParams(vmem_limit_bytes=16 << 20),
        cost_estimate=pl.CostEstimate(flops=GATHER_FLOPS, bytes_accessed=6_000_000, transcendentals=0),
        name="gather",
    )(*args)


def finish_kernel(pos_ref, mine_ref, recv0_ref, recv1_ref, share_ref, dk_ref, dv_ref):
    index, _, core = place()
    row = lax.broadcasted_iota(jnp.int32, (ROWS, HEAD), 0)
    first = pos_ref[2 * index] - index * ROWS
    second = pos_ref[2 * index + 1] - index * ROWS
    shares = []
    for source in range(2):
        share = share_ref[source].astype(F32)
        for i in range(1, share_ref.shape[0] // 2):
            share = share + share_ref[2 * i + source].astype(F32)
        shares.append(share)
    for half in range(2):
        which = core if half == 0 else 1 - core
        share = jnp.where(which == 0, shares[0], shares[1])
        for g in range(2):
            for i, out in enumerate((dk_ref, dv_ref)):
                at = 4 * g + 2 * i
                if half == 0:
                    total = mine_ref[:, (2 * g + i) * HEAD : (2 * g + i + 1) * HEAD]
                else:
                    total = (recv0_ref, recv1_ref)[g][:, i * HEAD : (i + 1) * HEAD].astype(F32)
                total = total + jnp.where(row == first, share[at : at + 1], 0.0)
                total = total + jnp.where(row == second, share[at + 1 : at + 2], 0.0)
                out[:, window((2 * which + g) * HEAD, HEAD)] = total.astype(BF)


def finish(*args):
    shape = jax.ShapeDtypeStruct
    return pl.pallas_call(
        finish_kernel,
        in_specs=[SM] + [VM] * 4,
        out_specs=[VM, VM],
        out_shape=[shape((ROWS, 512), BF), shape((ROWS, 512), BF)],
        compiler_params=pltpu.CompilerParams(vmem_limit_bytes=16 << 20),
        name="finish",
    )(*args)


def to_sibling(block):
    return lax.ppermute(block, "ctx", [(i, i ^ 1) for i in range(lax.axis_size("ctx"))])


def to_chip(block, hops, flip=0):
    size = lax.axis_size("ctx")
    return lax.ppermute(block, "ctx", [(i, ((i + 2 * hops) % size) ^ flip) for i in range(size)])


def exchange(block):
    return lax.all_to_all(block, "ctx", 0, 0, tiled=True)


def body(queries, keys, values, cotangent, summary_positions):
    kv_own, kv_send, blocks, qd_send = pack(summary_positions, keys, values, queries, cotangent)
    kv_recv = to_sibling(kv_send)
    qd = to_sibling(qd_send)
    summ = exchange(blocks).reshape(1024, HEAD)
    kv0 = [jnp.concatenate([kv_own[g], kv_recv[g]], 0) for g in range(2)]
    kv1 = [to_chip(kv0[g], 1) for g in range(2)]
    kv2 = [to_chip(kv0[g], 2) for g in range(2)]
    sk0, sk1, pos = unpack(summary_positions.reshape(2, 128), summ)
    outs = attend(0, pos, queries, cotangent, qd, kv2[0], kv1[0], kv0[0], sk0)
    dq0, dqs0, summ_grad, own0, back1, back2 = outs
    back1_0, back2_0 = to_chip(back1, -1), to_chip(back2, -2)
    outs = attend(1, pos, queries, cotangent, qd, kv2[1], kv1[1], kv0[1], sk1, summ_grad, own0, dq0)
    outs, back1_0, back2_0, dqs0 = lax.optimization_barrier((outs, back1_0, back2_0, dqs0))
    dq_own, dqs1, summ_grad, own, back1, back2 = outs
    back1_1, back2_1 = to_chip(back1, -1), to_chip(back2, -2)
    mine, theirs0, theirs1, query_grad = gather(
        own, back1_0, back2_0, back1_1, back2_1, dq_own, to_sibling(dqs0), to_sibling(dqs1)
    )
    shares = exchange(summ_grad.reshape(128, 8, HEAD))
    key_grad, value_gradient = finish(
        summary_positions, mine, to_sibling(theirs0), to_sibling(theirs1), shares
    )
    return query_grad, key_grad, value_gradient


def solution(mesh):
    return jax.shard_map(
        body,
        mesh=mesh,
        in_specs=(P("ctx", None), P("ctx", None), P("ctx", None), P("ctx", None), P()),
        out_specs=(P("ctx", None), P("ctx", None), P("ctx", None)),
        check_vma=False,
    )
```

```python
import functools

import jax
import jax.numpy as jnp
from jax import lax
from jax.experimental import pallas as pl
from jax.experimental.pallas import tpu as pltpu
from jax.sharding import PartitionSpec as P

HEAD = 128
ROWS = 256
SPAN = 1792
GATHER_FLOPS = 6_000_000_000
UNPACK_FLOPS = 40_000_000_000
BIG = 3e38
NEG = -1e30
SCALE = HEAD**-0.5
LOG2E = 1.4426950408889634
F32 = jnp.float32
BF = jnp.bfloat16
VM = pl.BlockSpec(memory_space=pltpu.VMEM)
SM = pl.BlockSpec(memory_space=pltpu.SMEM)
HBM = pl.BlockSpec(memory_space=pltpu.HBM)
ANY = pl.BlockSpec(memory_space=pl.ANY)


def dot(a, b):
    return jnp.dot(a, b, preferred_element_type=F32)


def place():
    index = lax.axis_index("ctx")
    return index, index // 2, index % 2


def window(start, size):
    return pl.ds(pl.multiple_of(start, size), size)


def run(copies):
    for copy in copies:
        copy.start()
    for copy in copies:
        copy.wait()


def pack_kernel(
    pos_ref, k_hbm, v_hbm, q_hbm, d_hbm, own_hbm, send_hbm, block_hbm, qd_hbm,
    k_ref, v_ref, own_ref, send_ref, block_ref, qd_ref, sem, out_sem,
):
    index, _, core = place()
    outs = []

    def send(src, dst):
        outs.append(pltpu.make_async_copy(src, dst, out_sem.at[len(outs)]))
        outs[-1].start()

    loads = [pltpu.make_async_copy(k_hbm, k_ref, sem.at[0]), pltpu.make_async_copy(v_hbm, v_ref, sem.at[1])]
    for i, ref in enumerate((q_hbm, d_hbm)):
        src = ref.at[:, window((1 - core) * 1024, 1024)]
        loads.append(pltpu.make_async_copy(src, qd_ref.at[i], sem.at[2 + i]))
    for load in loads:
        load.start()
    loads[0].wait()
    loads[1].wait()
    for out, hbm, which in ((send_ref, send_hbm, 1 - core), (own_ref, own_hbm, core)):
        for g in range(2):
            cols = window((2 * which + g) * HEAD, HEAD)
            out[g, :, :HEAD] = k_ref[:, cols]
            out[g, :, HEAD:] = v_ref[:, cols]
        send(out, hbm)
    slot = lax.broadcasted_iota(jnp.int32, (8, ROWS), 0)
    row = lax.broadcasted_iota(jnp.int32, (8, ROWS), 1)
    first = pos_ref[2 * index] - index * ROWS
    second = pos_ref[2 * index + 1] - index * ROWS
    wanted = jnp.where(slot % 2 == 0, first, second)
    tiles = []
    for which in range(2):
        tile = jnp.zeros((8, HEAD), F32)
        for g in range(2):
            for i, ref in enumerate((k_ref, v_ref)):
                pick = ((row == wanted) & (slot // 2 == 2 * g + i)).astype(F32).astype(BF)
                head = 2 * which + g
                tile = tile + dot(pick, ref[:, head * HEAD : (head + 1) * HEAD])
        tiles.append(tile.astype(BF))
    for device in range(block_ref.shape[0]):
        block_ref[device] = tiles[device % 2]
    send(block_ref, block_hbm)
    for i in range(2):
        loads[2 + i].wait()
        send(qd_ref.at[i], qd_hbm.at[:, i * 1024 : (i + 1) * 1024])
    for done in outs:
        done.wait()


def pack(pos, keys, values, queries, cotangent):
    shape = jax.ShapeDtypeStruct
    return pl.pallas_call(
        pack_kernel,
        in_specs=[SM, HBM, HBM, HBM, HBM],
        out_specs=[HBM] * 4,
        out_shape=[
            shape((2, ROWS, 2 * HEAD), BF),
            shape((2, ROWS, 2 * HEAD), BF),
            shape((128, 8, HEAD), BF),
            shape((ROWS, 2048), BF),
        ],
        scratch_shapes=[
            pltpu.VMEM((ROWS, 512), BF),
            pltpu.VMEM((ROWS, 512), BF),
            pltpu.VMEM((2, ROWS, 256), BF),
            pltpu.VMEM((2, ROWS, 256), BF),
            pltpu.VMEM((128, 8, HEAD), BF),
            pltpu.VMEM((2, ROWS, 1024), BF),
            pltpu.SemaphoreType.DMA((4,)),
            pltpu.SemaphoreType.DMA((5,)),
        ],
        compiler_params=pltpu.CompilerParams(vmem_limit_bytes=60 << 20),
        name="pack",
    )(pos, keys, values, queries, cotangent)


def unpack_kernel(pos_ref, summ_ref, sk0_ref, sk1_ref, posb_ref, f_sc, t_sc):
    f_sc[...] = summ_ref[...].astype(F32)
    for g, out in enumerate((sk0_ref, sk1_ref)):
        for i in range(2):
            for r in range(2):
                slots = pl.ds(4 * g + 2 * i + r, 128, stride=8)
                t_sc[pl.ds(r, 128, stride=2), :] = f_sc[slots, :]
            out[:, i * HEAD : (i + 1) * HEAD] = t_sc[...].astype(BF)
    for i in range(2):
        row = jnp.broadcast_to(pos_ref[i : i + 1, :].astype(F32), (HEAD, HEAD))
        posb_ref[i * HEAD : (i + 1) * HEAD, :] = row.T


def unpack(pos, summ):
    shape = jax.ShapeDtypeStruct
    return pl.pallas_call(
        unpack_kernel,
        in_specs=[VM, VM],
        out_specs=[VM] * 3,
        out_shape=[shape((ROWS, 256), BF), shape((ROWS, 256), BF), shape((ROWS, HEAD), F32)],
        scratch_shapes=[pltpu.VMEM((1024, HEAD), F32), pltpu.VMEM((ROWS, HEAD), F32)],
        compiler_params=pltpu.CompilerParams(vmem_limit_bytes=16 << 20),
        cost_estimate=pl.CostEstimate(flops=UNPACK_FLOPS, bytes_accessed=1_000_000, transcendentals=0),
        name="unpack",
    )(pos, summ)


def fold(x, op):
    return op(x.reshape(x.shape[0] // 8, 8, x.shape[1]), axis=0)


def attend_kernel(g, pos_ref, q_hbm, d_hbm, qd_hbm, kv2, kv1, kv0, summ, *rest):
    before, rest = (rest[:3], rest[3:]) if g else (None, rest)
    dqo_hbm, dqs_hbm, gs_hbm, grad_hbm = rest[0], rest[1], rest[2], rest[3:6]
    (k_sc, v_sc, kt_sc, vt_sc, s_sc, q_sc, d_sc, dq_sc, dk_sc, dv_sc, lim_sc, lims_sc) = rest[6:18]
    own_sc, bf_sc, gs_sc, gsb_sc, dq_before, sem, out_sem = rest[18:]
    _, chip, core = place()
    mine = window(core * ROWS, ROWS)
    theirs = window((1 - core) * ROWS, ROWS)
    copies = []

    def copy(src, dst):
        copies.append(pltpu.make_async_copy(src, dst, sem.at[len(copies)]))
        copies[-1].start()

    if g:
        copy(before[0], gs_sc)
        copy(before[1], own_sc.at[:, :256])
        copy(before[2], dq_before)
    copy(q_hbm.at[:, window(core * 1024 + g * 512, 512)], q_sc.at[mine])
    copy(d_hbm.at[:, window(core * 1024 + g * 512, 512)], d_sc.at[mine])
    copy(qd_hbm.at[:, g * 512 : (g + 1) * 512], q_sc.at[theirs])
    copy(qd_hbm.at[:, 1024 + g * 512 : 1536 + g * 512], d_sc.at[theirs])
    for i, kv in enumerate((kv2, kv1, kv0)):
        for part in range(2):
            at = window(i * 512 + (core if part == 0 else 1 - core) * ROWS, ROWS)
            rows = slice(part * ROWS, (part + 1) * ROWS)
            copy(kv.at[rows, :HEAD], k_sc.at[at])
            copy(kv.at[rows, HEAD:], v_sc.at[at])
    copy(summ.at[:, :HEAD], k_sc.at[1536:])
    copy(summ.at[:, HEAD:], v_sc.at[1536:])
    ki = lax.broadcasted_iota(jnp.int32, (ROWS, ROWS), 0)
    qi = lax.broadcasted_iota(jnp.int32, (ROWS, ROWS), 1)
    pos = jnp.concatenate([pos_ref[...], pos_ref[...]], 1)
    for b in range(2):
        lim_sc[b] = jnp.where((ki > qi) & (chip * 2 + b >= 4), BIG, NEG)
        lims_sc[b] = jnp.where(pos <= ((chip * 2 + b) * ROWS + qi).astype(F32), BIG, NEG)
    lim_sc[2] = jnp.where(ki <= qi, BIG, NEG)
    for done in copies:
        done.wait()
    for i in range(7):
        at = slice(i * ROWS, (i + 1) * ROWS)
        kt_sc[:, at] = k_sc[at, :].T
        vt_sc[:, at] = v_sc[at, :].T
    outs = []

    def send(src, dst):
        outs.append(pltpu.make_async_copy(src, dst, out_sem.at[len(outs)]))
        outs[-1].start()

    def emit():
        if g:
            send(dq_before, dqo_hbm.at[:, :512])
            send(dq_sc.at[mine], dqo_hbm.at[:, 512:])
        else:
            send(dq_sc.at[mine], dqo_hbm)
        send(dq_sc.at[theirs], dqs_hbm)
        dk_sc[1536:, :] = dk_sc[1536:, :] * SCALE
        for i, acc in enumerate((dk_sc, dv_sc)):
            for r in range(2):
                slots = pl.ds(4 * g + 2 * i + r, 128, stride=8)
                gs_sc[slots, :] = acc[pl.ds(1536 + r, 128, stride=2), :]
        if g:
            gsb_sc[...] = gs_sc[...].astype(BF)
        send(gsb_sc if g else gs_sc, gs_hbm)
        for i, hbm in enumerate(grad_hbm):
            for part in range(2):
                at = window((2 - i) * 512 + (core if part == 0 else 1 - core) * ROWS, ROWS)
                rows = slice(part * ROWS, (part + 1) * ROWS)
                stage, kind = (own_sc.at[:, g * 256 :], F32) if i == 0 else (bf_sc.at[i - 1], BF)
                stage[rows, :HEAD] = (dk_sc[at, :] * SCALE).astype(kind)
                stage[rows, HEAD:] = dv_sc[at, :].astype(kind)
            send(own_sc if i == 0 else stage, hbm)

    factor = SCALE * LOG2E

    def base(u, t):
        return 1536 if t == 5 else (u["b"] + t) * ROWS

    units = [dict(b=u // 4, h=u % 4, slot=u % 3) for u in range(8)]

    def open_unit(u):
        rows = slice(u["b"] * ROWS, (u["b"] + 1) * ROWS)
        cols = slice(u["h"] * HEAD, (u["h"] + 1) * HEAD)
        u["q"], u["d"] = q_sc[rows, cols], d_sc[rows, cols]
        u["qt"], u["dt"] = u["q"].T, u["d"].T
        u["m"] = u["l"] = u["o"] = u["dq"] = None

    def scores(u, t):
        b, at = u["b"], slice(t * ROWS, (t + 1) * ROWS)
        s = dot(k_sc[base(u, t) : base(u, t) + ROWS, :], u["qt"])
        if t == 0:
            limit = lim_sc[b]
        elif t == 4:
            limit = lim_sc[2]
        elif t == 5:
            limit = lims_sc[b]
        else:
            limit = jnp.where(chip * 2 + b + t >= 4, BIG, NEG)
        s = jnp.minimum(s, limit)
        s_sc[u["slot"], at, :] = s
        m = fold(s, jnp.max)
        u["m"] = m if u["m"] is None else jnp.maximum(u["m"], m)

    def close_scores(u):
        u["m2"] = jnp.max(u["m"], axis=0, keepdims=True) * factor

    def weights(u, t):
        b, at = u["b"], slice(t * ROWS, (t + 1) * ROWS)
        p = jnp.exp2(s_sc[u["slot"], at, :] * factor - u["m2"])
        s_sc[u["slot"], at, :] = p
        part = fold(p, jnp.sum)
        u["l"] = part if u["l"] is None else u["l"] + part
        o = dot(vt_sc[:, base(u, t) : base(u, t) + ROWS], p.astype(BF))
        u["o"] = o if u["o"] is None else u["o"] + o

    def close_weights(u):
        u["inv"] = 1.0 / jnp.sum(u["l"], axis=0, keepdims=True)
        attended = (u["o"] * u["inv"]).astype(BF).astype(F32)
        u["delta"] = jnp.sum(u["dt"].astype(F32) * attended, axis=0, keepdims=True)

    def grads(u, t):
        b, at = u["b"], slice(t * ROWS, (t + 1) * ROWS)
        keys = slice(base(u, t), base(u, t) + ROWS)
        dp = dot(v_sc[keys, :], u["dt"])
        p = s_sc[u["slot"], at, :] * u["inv"]
        ds = (p * (dp - u["delta"])).astype(BF)
        dk, dv = dot(ds, u["q"]), dot(p.astype(BF), u["d"])
        if u["h"] == 0 and (u["b"] == 0 or t == 4):
            dk_sc[keys, :] = dk
            dv_sc[keys, :] = dv
        else:
            dk_sc[keys, :] += dk
            dv_sc[keys, :] += dv
        dq = dot(kt_sc[:, keys], ds)
        u["dq"] = dq if u["dq"] is None else u["dq"] + dq

    def close_grads(u):
        rows = slice(u["b"] * ROWS, (u["b"] + 1) * ROWS)
        cols = slice(u["h"] * HEAD, (u["h"] + 1) * HEAD)
        dq_sc[rows, cols] = (u["dq"] * SCALE).T.astype(BF)

    for step in range(len(units) + 2):
        now, before, earlier = step < 8, 0 <= step - 1 < 8, 0 <= step - 2 < 8
        if now:
            open_unit(units[step])
        for t in range(6):
            if earlier:
                grads(units[step - 2], t)
            if before:
                weights(units[step - 1], t)
            if now:
                scores(units[step], t)
        if now:
            close_scores(units[step])
        if before:
            close_weights(units[step - 1])
        if earlier:
            close_grads(units[step - 2])
    emit()
    for done in outs:
        done.wait()


def attend(g, *args):
    shape = jax.ShapeDtypeStruct
    return pl.pallas_call(
        functools.partial(attend_kernel, g),
        in_specs=[VM, HBM, HBM] + [ANY] * (5 + 3 * g),
        out_specs=[HBM] * 6,
        out_shape=[
            shape((ROWS, 512 + 512 * g), BF),
            shape((ROWS, 512), BF),
            shape((1024, HEAD), BF if g else F32),
            shape((512, 256 + 256 * g), F32),
            shape((512, 256), BF),
            shape((512, 256), BF),
        ],
        scratch_shapes=[
            pltpu.VMEM((SPAN, HEAD), BF),
            pltpu.VMEM((SPAN, HEAD), BF),
            pltpu.VMEM((HEAD, SPAN), BF),
            pltpu.VMEM((HEAD, SPAN), BF),
            pltpu.VMEM((3, 1536, ROWS), F32),
            pltpu.VMEM((512, 512), BF),
            pltpu.VMEM((512, 512), BF),
            pltpu.VMEM((512, 512), BF),
            pltpu.VMEM((SPAN, HEAD), F32),
            pltpu.VMEM((SPAN, HEAD), F32),
            pltpu.VMEM((3, ROWS, ROWS), F32),
            pltpu.VMEM((2, ROWS, ROWS), F32),
            pltpu.VMEM((512, 256 + 256 * g), F32),
            pltpu.VMEM((2, 512, 256), BF),
            pltpu.VMEM((1024, HEAD), F32),
            pltpu.VMEM((1024, HEAD), BF),
            pltpu.VMEM((ROWS, 512), BF),
            pltpu.SemaphoreType.DMA((24,)),
            pltpu.SemaphoreType.DMA((8,)),
        ],
        compiler_params=pltpu.CompilerParams(vmem_limit_bytes=24 << 20),
        cost_estimate=pl.CostEstimate(
            flops=5_000_000_000, bytes_accessed=4_000_000, transcendentals=3_000_000
        ),
        name="attend",
    )(*args)


def gather_kernel(own, b10, b20, b11, b21, dq_own, dqr0, dqr1, mine_ref, their0, their1, dq_ref):
    core = place()[2]
    for g, (back1, back2, their) in enumerate(((b10, b20, their0), (b11, b21, their1))):
        cols = slice(g * 256, (g + 1) * 256)
        total = own[:, cols] + back1[...].astype(F32) + back2[...].astype(F32)
        mine_ref[:, cols] = total[:ROWS].astype(BF)
        their[...] = total[ROWS:].astype(BF)
        dq_ref[:, window(((1 - core) * 2 + g) * 512, 512)] = (dqr0, dqr1)[g][...]
    dq_ref[:, window(core * 1024, 1024)] = dq_own[...]


def gather(*args):
    shape = jax.ShapeDtypeStruct
    return pl.pallas_call(
        gather_kernel,
        in_specs=[VM] * 8,
        out_specs=[VM] * 4,
        out_shape=[
            shape((ROWS, 512), BF),
            shape((ROWS, 256), BF),
            shape((ROWS, 256), BF),
            shape((ROWS, 2048), BF),
        ],
        compiler_params=pltpu.CompilerParams(vmem_limit_bytes=16 << 20),
        cost_estimate=pl.CostEstimate(flops=GATHER_FLOPS, bytes_accessed=6_000_000, transcendentals=0),
        name="gather",
    )(*args)


def finish_kernel(pos_ref, mine_ref, recv0_ref, recv1_ref, share_ref, dk_ref, dv_ref):
    index, _, core = place()
    row = lax.broadcasted_iota(jnp.int32, (ROWS, HEAD), 0)
    first = pos_ref[2 * index] - index * ROWS
    second = pos_ref[2 * index + 1] - index * ROWS
    shares = []
    for source in range(2):
        share = share_ref[source].astype(F32)
        for i in range(1, share_ref.shape[0] // 2):
            share = share + share_ref[2 * i + source].astype(F32)
        shares.append(share)
    for half in range(2):
        which = core if half == 0 else 1 - core
        share = jnp.where(which == 0, shares[0], shares[1])
        for g in range(2):
            for i, out in enumerate((dk_ref, dv_ref)):
                at = 4 * g + 2 * i
                if half == 0:
                    total = mine_ref[:, (2 * g + i) * HEAD : (2 * g + i + 1) * HEAD].astype(F32)
                else:
                    total = (recv0_ref, recv1_ref)[g][:, i * HEAD : (i + 1) * HEAD].astype(F32)
                total = total + jnp.where(row == first, share[at : at + 1], 0.0)
                total = total + jnp.where(row == second, share[at + 1 : at + 2], 0.0)
                out[:, window((2 * which + g) * HEAD, HEAD)] = total.astype(BF)


def finish(*args):
    shape = jax.ShapeDtypeStruct
    return pl.pallas_call(
        finish_kernel,
        in_specs=[SM] + [VM] * 4,
        out_specs=[VM, VM],
        out_shape=[shape((ROWS, 512), BF), shape((ROWS, 512), BF)],
        compiler_params=pltpu.CompilerParams(vmem_limit_bytes=16 << 20),
        name="finish",
    )(*args)


def to_sibling(block):
    return lax.ppermute(block, "ctx", [(i, i ^ 1) for i in range(lax.axis_size("ctx"))])


def to_chip(block, hops, flip=0):
    size = lax.axis_size("ctx")
    return lax.ppermute(block, "ctx", [(i, ((i + 2 * hops) % size) ^ flip) for i in range(size)])


def exchange(block):
    return lax.all_to_all(block, "ctx", 0, 0, tiled=True)


def body(queries, keys, values, cotangent, summary_positions):
    kv_own, kv_send, blocks, qd_send = pack(summary_positions, keys, values, queries, cotangent)
    kv_recv = to_sibling(kv_send)
    qd = to_sibling(qd_send)
    summ = exchange(blocks).reshape(1024, HEAD)
    kv0 = [jnp.concatenate([kv_own[g], kv_recv[g]], 0) for g in range(2)]
    kv1 = [to_chip(kv0[g], 1) for g in range(2)]
    kv2 = [to_chip(kv0[g], 2) for g in range(2)]
    sk0, sk1, pos = unpack(summary_positions.reshape(2, 128), summ)
    outs = attend(0, pos, queries, cotangent, qd, kv2[0], kv1[0], kv0[0], sk0)
    dq0, dqs0, summ_grad, own0, back1, back2 = outs
    back1_0, back2_0 = to_chip(back1, -1), to_chip(back2, -2)
    outs = attend(1, pos, queries, cotangent, qd, kv2[1], kv1[1], kv0[1], sk1, summ_grad, own0, dq0)
    outs, back1_0, back2_0, dqs0 = lax.optimization_barrier((outs, back1_0, back2_0, dqs0))
    dq_own, dqs1, summ_grad, own, back1, back2 = outs
    back1_1, back2_1 = to_chip(back1, -1), to_chip(back2, -2)
    mine, theirs0, theirs1, query_grad = gather(
        own, back1_0, back2_0, back1_1, back2_1, dq_own, to_sibling(dqs0), to_sibling(dqs1)
    )
    shares = exchange(summ_grad.reshape(128, 8, HEAD))
    key_grad, value_gradient = finish(
        summary_positions, mine, to_sibling(theirs0), to_sibling(theirs1), shares
    )
    return query_grad, key_grad, value_gradient


def solution(mesh):
    return jax.shard_map(
        body,
        mesh=mesh,
        in_specs=(P("ctx", None), P("ctx", None), P("ctx", None), P("ctx", None), P()),
        out_specs=(P("ctx", None), P("ctx", None), P("ctx", None)),
        check_vma=False,
    )
```
